32 devices in a mesh: comp: 2 (over y), gx: 4 (over x, core), gy: 4 (over z).
Axes of the slice: x: 2, y: 2, z: 4, core: 2. Of those that a mesh axis runs over, the one named last changes fastest.
Arguments:
- state: float32 [2, 30, 128, 1024], P('comp', None, 'gx', 'gy'), may hold values from -6 to 6
- conduct: float32 [2, 30, 128, 1024], P('comp', None, 'gx', 'gy'), may hold values from 0.3 to 3
- storage: float32 [2], P('comp'), may hold values from 0.05 to 0.5
- surface_source: float32 [2, 128, 1024], P('comp', 'gx', 'gy'), may hold values from -6 to 6
- plant_type: int32 [2, 128, 1024], P('comp', 'gx', 'gy'), may hold values from 0 to 15
- plant_table: float32 [16, 2], replicated, may hold values from 0.3 to 3
- layer_weights: float32 [2, 16, 6], replicated, may hold values from 0.05 to 1
- remap_rows: int32 [2, 128], P('comp', 'gx'), may hold values from 0 to 31
- remap_weights: float32 [2, 1024, 128], P('comp', 'gy'), may hold values from 0 to 1
Outputs:
- new_state: float32 [2, 30, 128, 1024], P('comp', None, 'gx', 'gy')
- exchange_flux: float32 [2, 128, 1024], P('comp', 'gx', 'gy')
The draws below stay inside these ranges and needn't reach their ends.
All inputs are finite; a program needn't handle non-finite values.
Results may differ from the reference program's by a relative error of at most 0.0003.
Values sent between devices are 32-bit elements; how exact they have to be, the bound alone decides.
No kernel may reach another device: no remote copies, remote signals or barrier semaphores. Data moves between devices by JAX's collectives and lax.ppermute only.
A program may use at most 64 MiB of HBM per device.

```python
import math
import jax
import jax.numpy as jnp
from jax import lax

CX = 32
LV = 30
NS = 6
PATCH = 128
PLANTS = 16
ITERS = 3
NX = 128
NY = 1024


def draw_remap_weights(key, part):
    key_diag, key_off = jax.random.split(key)
    column = jnp.arange(NY) % PATCH
    eye = column[:, None] == jnp.arange(PATCH)[None, :]
    diag = jax.random.uniform(key_diag, (2, NY, 1), jnp.float32, 0.5, 1.0)
    off = jax.random.uniform(key_off, (2, NY, PATCH), jnp.float32, 0.0, 1.0) * (0.6 / PATCH)
    return jnp.where(eye[None], diag, off).astype(jnp.float32)


def place_ends(drawn, stream_key, least, top_value):
    index_at = [jax.random.randint(jax.random.fold_in(stream_key, axis), (), 0, length) for axis, length in enumerate(drawn.shape)]
    main_axis = drawn.shape.index(max(drawn.shape))
    next_to = index_at[:main_axis] + [(index_at[main_axis] + 1) % drawn.shape[main_axis]] + index_at[main_axis + 1:]
    return drawn.at[tuple(index_at)].set(least).at[tuple(next_to)].set(top_value)


def levels(key, dims, cuts, low, high):
    def one(axis_at, shards_of):
        heights = jax.random.uniform(jax.random.fold_in(jax.random.fold_in(key, 6), axis_at), (shards_of,), jnp.float32, low / len(cuts), high / len(cuts))
        return jnp.repeat(jnp.exp(heights), dims[axis_at] // shards_of).reshape((-1,) + (1,) * (len(dims) - axis_at - 1))

    gain = one(*cuts[0])
    for cut in cuts[1:]:
        gain = gain * one(*cut)
    return gain


def gaussian(stream_key, dims, width, bound, cuts=(), dtype=jnp.bfloat16):
    loudness = levels(stream_key, dims, cuts, -0.22, 0.18) if cuts else 1.0
    drawn = jax.random.normal(stream_key, dims, jnp.float32) * width * loudness
    return jnp.minimum(jnp.maximum(drawn, -bound), bound).astype(dtype)


def setup_inputs(seed: int = 0) -> dict:
    streams_of = jax.random.split(jax.random.key(seed), 10)
    state = gaussian(streams_of[0], (2, LV, NX, NY), 1.0, 6.0, ((0, 2), (2, 4), (3, 4)), jnp.float32)
    conduct = jnp.clip(jnp.exp(math.log(3.0) - 2.3025851 * jax.random.uniform(streams_of[1], (2, LV, NX, NY), jnp.float32) ** levels(streams_of[1], (2, LV, NX, NY), ((0, 2), (2, 4), (3, 4)), -0.2, 0.2)), 0.3, 3.0)
    storage = jnp.clip(jnp.exp(math.log(0.5) - 2.3025851 * jax.random.uniform(streams_of[2], (2,), jnp.float32) ** levels(streams_of[2], (2,), ((0, 2),), -0.2, 0.2)), 0.05, 0.5)
    surface_source = gaussian(streams_of[3], (2, NX, NY), 1.0, 6.0, ((0, 2), (1, 4), (2, 4)), jnp.float32)
    plant_type = place_ends(jax.random.randint(streams_of[4], (2, NX, NY), 0, PLANTS), jax.random.fold_in(streams_of[4], 1), 0, PLANTS - 1).astype(jnp.int32)
    plant_table = jnp.clip(jnp.exp(jax.random.uniform(streams_of[5], (PLANTS, 2), jnp.float32, math.log(0.3), math.log(3.0))), 0.3, 3.0)
    layer_weights = jnp.clip(jax.random.uniform(streams_of[6], (2, PLANTS, NS), jnp.float32, 0.05, 1.0), 0.05, 1.0)
    remap_rows = place_ends(jax.random.randint(streams_of[7], (2, NX), 0, CX), jax.random.fold_in(streams_of[7], 1), 0, CX - 1).astype(jnp.int32)
    remap_weights = draw_remap_weights(jax.random.fold_in(streams_of[9], 71), 0)
    return dict(state=state, conduct=conduct, storage=storage, surface_source=surface_source, plant_type=plant_type, plant_table=plant_table, layer_weights=layer_weights, remap_rows=remap_rows, remap_weights=remap_weights)


def apply_padded(vp, kp):
    v = vp[1:-1, 1:-1, 1:-1]
    kc = kp[1:-1, 1:-1, 1:-1]
    total = jnp.zeros_like(v)
    moves = [(2, 1, 1), (0, 1, 1), (1, 2, 1), (1, 0, 1), (1, 1, 2), (1, 1, 0)]
    for a, b, e in moves:
        vn = vp[a:a + v.shape[0], b:b + v.shape[1], e:e + v.shape[2]]
        kn = kp[a:a + v.shape[0], b:b + v.shape[1], e:e + v.shape[2]]
        total = total + 0.5 * (kc + kn) * (v - vn)
    return total

def least_squares(hmat, beta):
    gram = lax.optimization_barrier(jnp.sum(hmat[:, :, None] * hmat[:, None, :], axis=0))
    target_vector = beta * hmat[0, :]
    factor = jnp.linalg.cholesky(gram)
    return jax.scipy.linalg.cho_solve((factor, True), target_vector)

def reference(state, conduct, storage, surface_source, plant_type, plant_table, layer_weights, remap_rows, remap_weights):
    hp = lax.Precision.HIGHEST
    outs_state = []
    outs_flux = []
    for c in range(2):
        d = 1 - c
        rows = jnp.arange(NX) // CX * CX + remap_rows[c]
        src = state[d, :NS][:, rows, :]
        blocks = src.reshape(NS, NX, NY // PATCH, PATCH)
        wblk = remap_weights[c].reshape(NY // PATCH, PATCH, PATCH)
        remapped = jnp.einsum('lxbk,bjk->lxbj', blocks, wblk, precision=hp).reshape(NS, NX, NY)
        kinds = plant_type[c]
        own_prof = jnp.transpose(layer_weights[c][kinds], (2, 0, 1))
        other_prof = jnp.transpose(layer_weights[d][kinds], (2, 0, 1))
        own_force = lax.optimization_barrier(jnp.sum(own_prof * state[c, :NS], axis=0))
        other_force = lax.optimization_barrier(jnp.sum(other_prof * remapped, axis=0))
        if c == 0:
            atmospheric_forcing, soil_force = (own_force, other_force)
        else:
            atmospheric_forcing, soil_force = (other_force, own_force)
        params = plant_table[kinds]
        flux = params[:, :, 0] * (params[:, :, 1] * soil_force - atmospheric_forcing)
        sign = 1.0 - 2.0 * c
        top = sign * flux[None] * own_prof
        source = jnp.concatenate([top, jnp.zeros((LV - NS, NX, NY), jnp.float32)], axis=0)
        source = source.at[0].add(surface_source[c])
        field = state[c]
        keff = conduct[c] * (1.0 + 0.5 * jnp.tanh(field))
        kpad = jnp.pad(keff, 1)
        rhs = source - apply_padded(jnp.pad(field, 1), kpad)
        diagonal_shift = storage[c]
        beta = jnp.sqrt(jnp.sum(rhs * rhs))
        basis = [rhs / beta]
        hmat = jnp.zeros((ITERS + 1, ITERS), jnp.float32)
        for j in range(ITERS):
            krylov_vector = diagonal_shift * basis[j] + apply_padded(jnp.pad(basis[j], 1), kpad)
            for i in range(j + 1):
                h = jnp.sum(krylov_vector * basis[i])
                krylov_vector = krylov_vector - h * basis[i]
                hmat = hmat.at[i, j].set(h)
            nrm = jnp.sqrt(jnp.sum(krylov_vector * krylov_vector))
            hmat = hmat.at[j + 1, j].set(nrm)
            if j + 1 < ITERS:
                basis.append(krylov_vector / nrm)
        coef = least_squares(hmat, beta)
        update = field
        for j in range(ITERS):
            update = update + coef[j] * basis[j]
        outs_state.append(update)
        outs_flux.append(flux)
    return (jnp.stack(outs_state), jnp.stack(outs_flux))
```

```python
import jax
import jax.numpy as jnp
from jax import lax
from jax.experimental import pallas as pl
from jax.experimental.pallas import tpu as pltpu
from jax.sharding import PartitionSpec as P

NS = 6
PATCH = 128
PLANTS = 16
ITERS = 3
HALO = ITERS + 1
CENTRE = 8.0
LANES = 128
SUBLANES = 8
F32 = jnp.float32


def pairing(count, which):
    pairs = []
    for i in range(count):
        partner = i ^ 1 if which == 0 else (i + 1 if i % 2 else i - 1)
        pairs.append((i, partner if 0 <= partner < count else i))
    return pairs


def swap(value, axis, which):
    return lax.ppermute(value, axis, pairing(lax.axis_size(axis), which))


def iota(shape, dim):
    return lax.broadcasted_iota(jnp.int32, shape, dim)


VMEM_SPEC = pl.BlockSpec(memory_space=pltpu.VMEM)
SMEM_SPEC = pl.BlockSpec(memory_space=pltpu.SMEM)


def call(kernel, outs, ins, name, scratch=(), smem=()):
    specs = [SMEM_SPEC if i in smem else VMEM_SPEC for i in range(len(ins))]
    return pl.pallas_call(
        kernel,
        out_shape=[jax.ShapeDtypeStruct(s, F32) for s in outs],
        in_specs=specs,
        out_specs=[VMEM_SPEC] * len(outs),
        scratch_shapes=list(scratch),
        name=name,
    )(*ins)


def half_swap(v):
    return pltpu.roll(v, HALO, 0)


def pack_rows_kernel(meta, u_ref, k_ref, out0, out1):
    levels, rows, cols = u_ref.shape
    upper = iota((SUBLANES, cols), 0) < HALO

    def low(l):
        u = u_ref[l, :SUBLANES, :]
        k = k_ref[l, :SUBLANES, :]
        return jnp.where(upper, u, half_swap(k))

    def high(l):
        u = u_ref[l, rows - SUBLANES :, :]
        k = k_ref[l, rows - SUBLANES :, :]
        return jnp.where(upper, half_swap(u), k)

    odd = meta[1] % 2
    for parity in range(2):

        @pl.when(odd == parity)
        def _():
            for l in range(levels):
                a, b = (high(l), low(l)) if parity == 0 else (low(l), high(l))
                out0[l] = a
                out1[l] = b


def lookup(table, kinds):
    out = jnp.full(kinds.shape, table(0), F32)
    for p in range(1, PLANTS):
        out = jnp.where(kinds == p, table(p), out)
    return out


def split(v):
    hi = v.astype(jnp.bfloat16)
    lo = (v - hi.astype(F32)).astype(jnp.bfloat16)
    return hi, lo


def source_kernel(
    meta, rows_ref, table_ref, lw_ref, u_ref, part_ref, w_ref, kind_ref, surf_ref, flux_ref, src_ref, out0, out1, picked
):
    _, nx, ny = part_ref.shape
    comp = meta[0]
    for x in range(nx):
        r = rows_ref[0, x]
        picked[:, pl.ds(x, 1), :] = part_ref[:, pl.ds(r, 1), :]
    kinds = kind_ref[0]
    own = [lookup(lambda p: lw_ref[comp, p, l], kinds) for l in range(NS)]
    own_force = own[0] * u_ref[0, 0]
    for l in range(1, NS):
        own_force = own_force + own[l] * u_ref[0, l]
    other_prof = [lookup(lambda p: lw_ref[1 - comp, p, l], kinds) for l in range(NS)]
    forces = []
    for b in range(ny // PATCH):
        cols = slice(b * PATCH, (b + 1) * PATCH)
        x_hi, x_lo = split(picked[:, :, cols].reshape(NS * nx, PATCH))
        w_hi, w_lo = split(w_ref[0, cols, :])
        dims = (((1,), (1,)), ((), ()))
        y = lax.dot_general(x_hi, w_lo, dims, preferred_element_type=F32)
        y = y + lax.dot_general(x_lo, w_hi, dims, preferred_element_type=F32)
        y = y + lax.dot_general(x_hi, w_hi, dims, preferred_element_type=F32)
        y = y.reshape(NS, nx, PATCH)
        total = other_prof[0][:, cols] * y[0]
        for l in range(1, NS):
            total = total + other_prof[l][:, cols] * y[l]
        forces.append(total)
    other_force = jnp.concatenate(forces, axis=1)
    first = comp == 0
    atmos = jnp.where(first, own_force, other_force)
    soil = jnp.where(first, other_force, own_force)
    conductance = lookup(lambda p: table_ref[p, 0], kinds)
    factor = lookup(lambda p: table_ref[p, 1], kinds)
    flux = conductance * (factor * soil - atmos)
    flux_ref[0] = flux
    signed = jnp.where(first, flux, -flux)
    upper = iota((SUBLANES, ny), 0) < HALO
    odd = meta[1] % 2 == 1
    src = []
    for l in range(NS):
        s = signed * own[l]
        if l == 0:
            s = s + surf_ref[0]
        src_ref[l] = s
        src.append(s)
    for j in range(NS // 2):
        a, b = src[2 * j], src[2 * j + 1]
        low = jnp.where(upper, a[:SUBLANES], half_swap(b[:SUBLANES]))
        high = jnp.where(upper, half_swap(a[nx - SUBLANES :]), b[nx - SUBLANES :])
        out0[j] = jnp.where(odd, low, high)
        out1[j] = jnp.where(odd, high, low)


def pack_columns_kernel(meta, u_ref, k_ref, s_ref, x0, x1, s0, s1, halo_u, halo_k, halo_s, out0, out1):
    levels, nx, ny = u_ref.shape
    upper = iota((SUBLANES, ny), 0) < HALO
    gx, count = meta[1], meta[3]
    odd = gx % 2 == 1
    has_low, has_high = gx > 0, gx < count - 1
    keep = jnp.where(upper, jnp.where(has_high, 1.0, 0.0), jnp.where(has_low, 1.0, 0.0)) != 0.0

    def halves(first, second, j):
        a, b = first[j], second[j]
        high, low = jnp.where(odd, b, a), jnp.where(odd, a, b)
        one = jnp.where(upper, high, half_swap(low))
        two = jnp.where(upper, half_swap(high), low)
        return jnp.where(keep, one, 0.0), jnp.where(keep, two, 0.0)

    def level(l, _):
        u, k = halves(x0, x1, l)
        halo_u[l] = u
        halo_k[l] = k
        return 0

    lax.fori_loop(0, levels, level, 0, unroll=5)
    for j in range(NS // 2):
        a, b = halves(s0, s1, j)
        halo_s[2 * j] = a
        halo_s[2 * j + 1] = b

    group = iota((nx + 2 * HALO, LANES), 1) // HALO
    y_odd = meta[2] % 2

    def columns(main, halo, l, high):
        at = ny - LANES if high else 0
        tile = jnp.concatenate([main[l, :, at : at + LANES], halo[l, :, at : at + LANES]], axis=0)
        return tile

    for parity in range(2):

        @pl.when(y_odd == parity)
        def _():
            for f, (main, halo, n) in enumerate(((u_ref, halo_u, levels), (k_ref, halo_k, levels), (s_ref, halo_s, NS))):
                zero = jnp.zeros((nx + 2 * HALO, LANES), F32)
                first, second = zero, zero
                for l in range(n):
                    high = pltpu.roll(columns(main, halo, l, True), (HALO * l + HALO) % LANES, 1)
                    low = columns(main, halo, l, False)
                    low = pltpu.roll(low, HALO * l, 1) if l else low
                    a, b = (high, low) if parity == 0 else (low, high)
                    first = jnp.where(group == l, a, first)
                    second = jnp.where(group == l, b, second)
                out0[f] = first
                out1[f] = second


def chain_kernel(
    meta, storage_ref, u_ref, k_ref, s_ref, halo_u, halo_k, halo_s, y0, y1,
    r_out, p1_out, p2_out, moments,
    ext_a, ext_b, keff, cz, cx, cy, inside,
):
    levels, nx, ny = u_ref.shape
    rows, cols = nx + 2 * HALO, ny + LANES
    gx, gy, ngx, ngy = meta[1], meta[2], meta[3], meta[4]
    odd = gy % 2 == 1
    has_low, has_high = gy > 0, gy < ngy - 1
    lane = iota((rows, LANES), 1)
    keep_high = lane < jnp.where(has_high, HALO, 0)
    keep_low = lane >= jnp.where(has_low, LANES - HALO, LANES)

    row = iota((rows, cols), 0)
    col = iota((rows, cols), 1)
    ok = (row < nx) | ((row < nx + HALO) & (gx < ngx - 1)) | ((row >= nx + HALO) & (gx > 0))
    ok = ok & ((col < ny) | ((col < ny + HALO) & has_high) | ((col >= cols - HALO) & has_low))
    inside[...] = jnp.where(ok, 1.0, 0.0)

    def third(f, l):
        a, b = y0[f], y1[f]
        high, low = jnp.where(odd, b, a), jnp.where(odd, a, b)
        high = pltpu.roll(high, (LANES - HALO * l) % LANES, 1) if (HALO * l) % LANES else high
        low = pltpu.roll(low, (2 * LANES - HALO - HALO * l) % LANES, 1)
        return jnp.where(keep_high, high, jnp.where(keep_low, low, 0.0))

    def extend(main, halo, f, l):
        left = jnp.concatenate([main[l], halo[l]], axis=0)
        return jnp.concatenate([left, third(f, l)], axis=1)

    for l in range(levels):
        u = extend(u_ref, halo_u, 0, l)
        ext_a[l] = u
        keff[l] = extend(k_ref, halo_k, 1, l) * (1.0 + 0.5 * jnp.tanh(u))

    def faces(l, _):
        k = keff[l]
        below = keff[jnp.maximum(l - 1, 0)]
        cz[l] = 0.5 * jnp.where(l == 0, k, k + below)
        cx[l] = 0.5 * (k + pltpu.roll(k, rows - 1, 0))
        cy[l] = 0.5 * (k + pltpu.roll(k, cols - 1, 1))
        return 0

    lax.fori_loop(0, levels, faces, 0)
    cz[levels] = 0.5 * keff[levels - 1]

    def flux_sum(src, l, v, flow, xr, yr):
        nxt = src[jnp.minimum(l + 1, levels - 1), :xr, :yr]
        nxt = jnp.where(l == levels - 1, 0.0, nxt)
        up = cz[l + 1, :xr, :yr] * (v[:xr, :yr] - nxt)
        vx = v[:, :yr]
        fx = cx[l, :, :yr] * (vx - pltpu.roll(vx, rows - 1, 0))
        vy = v[:xr]
        fy = cy[l, :xr, :] * (vy - pltpu.roll(vy, cols - 1, 1))
        dx = fx - pltpu.roll(fx, 1, 0)
        dy = fy - pltpu.roll(fy, 1, 1)
        return (up - flow) + (dx[:xr] + dy[:, :yr]), up

    def fold(v):
        v = v[:, :LANES] + v[:, LANES:] if ny == 2 * LANES else sum(v[:, c : c + LANES] for c in range(0, ny, LANES))
        total = v[:SUBLANES]
        for r in range(SUBLANES, nx, SUBLANES):
            total = total + v[r : r + SUBLANES]
        return total

    zero_tile = jnp.zeros((SUBLANES, LANES), F32)

    def residual(l, carry):
        flow, m0 = carry
        v = ext_a[l]
        w, up = flux_sum(ext_a, l, v, flow, rows, cols)
        r = -w * inside[...]
        ext_b[l] = r
        return up, m0

    flow0 = -cz[0] * ext_a[0]
    lax.fori_loop(0, levels, residual, (flow0, zero_tile))
    for l in range(NS):
        ext_b[l] = ext_b[l] + extend(s_ref, halo_s, 2, l)

    def copy_out(l, m0):
        v = ext_b[l, :nx, :ny]
        r_out[l] = v
        return m0 + fold(v * v)

    m0 = lax.fori_loop(0, levels, copy_out, zero_tile)
    shift = storage_ref[0] - CENTRE

    def apply(src, dst, out):
        def step(l, carry):
            flow, cross, square = carry
            v = src[l]
            w, up = flux_sum(src, l, v, flow, rows, cols)
            w = (w + shift * v) * inside[...]
            dst[l] = w
            own = w[:nx, :ny]
            out[l] = own
            return up, cross + fold(own * v[:nx, :ny]), square + fold(own * own)

        return lax.fori_loop(0, levels, step, (-cz[0] * src[0], zero_tile, zero_tile))[1:]

    m1, m2 = apply(ext_b, ext_a, p1_out)
    m3, m4 = apply(ext_a, ext_b, p2_out)

    def last(l, carry):
        flow, cross, square = carry
        v = ext_b[l]
        w, up = flux_sum(ext_b, l, v, flow, nx, ny)
        own_v = v[:nx, :ny]
        own = w + shift * own_v
        return up, cross + fold(own * own_v), square + fold(own * own)

    first_flow = -cz[0, :nx, :ny] * ext_b[0, :nx, :ny]
    m5, m6 = lax.fori_loop(0, levels, last, (first_flow, zero_tile, zero_tile))[1:]
    which = iota((SUBLANES, LANES), 0)
    packed = zero_tile
    for i, m in enumerate((m0, m1, m2, m3, m4, m5, m6)):
        total = jnp.sum(jnp.sum(m, axis=1, keepdims=True), axis=0, keepdims=True)
        packed = jnp.where(which == i, total, packed)
    for d in range(moments.shape[0]):
        moments[d] = packed


def update_kernel(gathered, u_ref, r_ref, p1_ref, p2_ref, out):
    total = gathered[0]
    for d in range(1, gathered.shape[0]):
        total = total + gathered[d]
    m = [total[i : i + 1, :] for i in range(7)]
    theta = CENTRE

    def gram(i, j):
        return m[i + j + 2] + 2.0 * theta * m[i + j + 1] + theta * theta * m[i + j]

    b = [m[i + 1] + theta * m[i] for i in range(3)]
    l00 = jnp.sqrt(gram(0, 0))
    l10 = gram(1, 0) / l00
    l20 = gram(2, 0) / l00
    l11 = jnp.sqrt(gram(1, 1) - l10 * l10)
    l21 = (gram(2, 1) - l20 * l10) / l11
    l22 = jnp.sqrt(gram(2, 2) - l20 * l20 - l21 * l21)
    z0 = b[0] / l00
    z1 = (b[1] - l10 * z0) / l11
    z2 = (b[2] - l20 * z0 - l21 * z1) / l22
    c2 = z2 / l22
    c1 = (z1 - l21 * c2) / l11
    c0 = (z0 - l10 * c1 - l20 * c2) / l00
    levels, nx, ny = r_ref.shape
    wide = lambda c: jnp.broadcast_to(jnp.concatenate([c] * (ny // LANES), axis=1), (nx, ny))
    c0, c1, c2 = wide(c0), wide(c1), wide(c2)

    def step(l, _):
        out[0, l] = u_ref[0, l] + c0 * r_ref[l] + c1 * p1_ref[l] + c2 * p2_ref[l]
        return 0

    lax.fori_loop(0, levels, step, 0, unroll=2)


def body(
    state, conduct, storage, surface_source, plant_type, plant_table, layer_weights, remap_rows, remap_weights
):
    levels, nx, ny = state.shape[1:]
    ngx, ngy = lax.axis_size("gx"), lax.axis_size("gy")
    meta = jnp.stack(
        [lax.axis_index("comp"), lax.axis_index("gx"), lax.axis_index("gy"), jnp.int32(ngx), jnp.int32(ngy)]
    ).astype(jnp.int32)
    field, cond = state[0], conduct[0]
    partner = lax.ppermute(field[:NS], "comp", [(i, i ^ 1) for i in range(lax.axis_size("comp"))])
    x0, x1 = call(pack_rows_kernel, [(levels, SUBLANES, ny)] * 2, [meta, field, cond], "pack_rows", smem=(0,))
    x0, x1 = swap(x0, "gx", 0), swap(x1, "gx", 1)
    flux, src, s0, s1 = call(
        source_kernel,
        [(1, nx, ny), (NS, nx, ny)] + [(NS // 2, SUBLANES, ny)] * 2,
        [meta, remap_rows, plant_table, layer_weights, state, partner, remap_weights, plant_type, surface_source],
        "source",
        scratch=[pltpu.VMEM((NS, nx, ny), F32)],
        smem=(0, 1, 2, 3),
    )
    s0, s1 = swap(s0, "gx", 0), swap(s1, "gx", 1)
    rows, cols = nx + 2 * HALO, ny + LANES
    halo_u, halo_k, halo_s, y0, y1 = call(
        pack_columns_kernel,
        [(levels, SUBLANES, ny)] * 2 + [(NS, SUBLANES, ny)] + [(3, rows, LANES)] * 2,
        [meta, field, cond, src, x0, x1, s0, s1],
        "pack_columns",
        smem=(0,),
    )
    y0, y1 = swap(y0, "gy", 0), swap(y1, "gy", 1)
    group = ngx * ngy
    full = pltpu.VMEM((levels, rows, cols), F32)
    r, p1, p2, moments = call(
        chain_kernel,
        [(levels, nx, ny)] * 3 + [(group, SUBLANES, LANES)],
        [meta, storage, field, cond, src, halo_u, halo_k, halo_s, y0, y1],
        "chain",
        scratch=[full, full, full, pltpu.VMEM((levels + 1, rows, cols), F32), full, full, pltpu.VMEM((rows, cols), F32)],
        smem=(0, 1),
    )
    gathered = lax.all_to_all(moments, ("gx", "gy"), 0, 0)
    (new_state,) = call(update_kernel, [state.shape], [gathered, state, r, p1, p2], "update")
    return new_state, flux


def solution(mesh):
    in_specs = (
        P("comp", None, "gx", "gy"),
        P("comp", None, "gx", "gy"),
        P("comp"),
        P("comp", "gx", "gy"),
        P("comp", "gx", "gy"),
        P(),
        P(),
        P("comp", "gx"),
        P("comp", "gy", None),
    )
    out_specs = (P("comp", None, "gx", "gy"), P("comp", "gx", "gy"))
    return jax.shard_map(body, mesh=mesh, in_specs=in_specs, out_specs=out_specs, check_vma=False)
```

```python
import jax
import jax.numpy as jnp
from jax import lax
from jax.experimental import pallas as pl
from jax.experimental.pallas import tpu as pltpu
from jax.sharding import PartitionSpec as P

NS = 6
PATCH = 128
PLANTS = 16
ITERS = 3
HALO = ITERS + 1
CENTRE = 8.0
LANES = 128
SUB = 8
MOMENTS = 2 * ITERS + 1
PROFILES = 2 * NS + 3
F32 = jnp.float32
MIB = 1 << 20


def pairing(count, which):
    pairs = []
    for i in range(count):
        partner = i ^ 1 if which == 0 else (i + 1 if i % 2 else i - 1)
        pairs.append((i, partner if 0 <= partner < count else i))
    return pairs


def swap(value, axis, which):
    return lax.ppermute(value, axis, pairing(lax.axis_size(axis), which))


def everyone(value, axis):
    n = lax.axis_size(axis)
    return [value] + [lax.ppermute(value, axis, [(i, i ^ d) for i in range(n)]) for d in range(1, n)]


def iota(shape, dim):
    return lax.broadcasted_iota(jnp.int32, shape, dim)


VMEM_SPEC = pl.BlockSpec(memory_space=pltpu.VMEM)
SMEM_SPEC = pl.BlockSpec(memory_space=pltpu.SMEM)
HBM_SPEC = pl.BlockSpec(memory_space=pltpu.HBM)


def call(kernel, outs, ins, name, scratch=(), smem=(), hbm=(), hbm_outs=(), limit=2, alias=None):
    def spec(i):
        return SMEM_SPEC if i in smem else HBM_SPEC if i in hbm else VMEM_SPEC

    def place(i, v):
        if i in smem:
            return v
        return pltpu.with_memory_space_constraint(v, pltpu.HBM if i in hbm else pltpu.VMEM)

    return pl.pallas_call(
        kernel,
        out_shape=[jax.ShapeDtypeStruct(s, F32) if i in hbm_outs else pltpu.VMEM(s, F32) for i, s in enumerate(outs)],
        in_specs=[spec(i) for i in range(len(ins))],
        out_specs=[HBM_SPEC if i in hbm_outs else VMEM_SPEC for i in range(len(outs))],
        scratch_shapes=list(scratch),
        input_output_aliases=alias or {},
        name=name,
        compiler_params=pltpu.CompilerParams(vmem_limit_bytes=limit * MIB),
    )(*[place(i, v) for i, v in enumerate(ins)])


def half_swap(v):
    return pltpu.roll(v, HALO, 0)


def layers_kernel(u_hbm, layers, sem):
    copy = pltpu.make_async_copy(u_hbm.at[0, pl.ds(0, NS)], layers, sem)
    copy.start()
    copy.wait()


def edges_kernel(u_hbm, k_hbm, out0, out1, low_u, low_k, high_u, high_k, sems):
    _, levels, rows, cols = u_hbm.shape
    copies = [
        pltpu.make_async_copy(u_hbm.at[0, :, pl.ds(0, SUB)], low_u, sems.at[0]),
        pltpu.make_async_copy(k_hbm.at[0, :, pl.ds(0, SUB)], low_k, sems.at[1]),
        pltpu.make_async_copy(u_hbm.at[0, :, pl.ds(rows - SUB, SUB)], high_u, sems.at[2]),
        pltpu.make_async_copy(k_hbm.at[0, :, pl.ds(rows - SUB, SUB)], high_k, sems.at[3]),
    ]
    for c in copies:
        c.start()
    upper = iota((SUB, cols), 0) < HALO
    odd = lax.axis_index("gx") % 2 == 1
    for c in copies:
        c.wait()
    for l in range(levels):
        low = jnp.where(upper, low_u[l], half_swap(low_k[l]))
        high = jnp.where(upper, half_swap(high_u[l]), high_k[l])
        out0[l] = jnp.where(odd, low, high)
        out1[l] = jnp.where(odd, high, low)


def own_kernel(
    table_hbm, lw_hbm, u_hbm, k_hbm, kind_hbm, ext_u, ext_k, prof, table, lw, u_ref, k_ref, kind_ref, sems, field_sems
):
    _, levels, nx, ny = u_ref.shape
    tiles = ny // LANES
    comp = lax.axis_index("comp")
    small = [
        pltpu.make_async_copy(table_hbm, table, sems.at[0]),
        pltpu.make_async_copy(lw_hbm, lw, sems.at[1]),
        pltpu.make_async_copy(kind_hbm, kind_ref, sems.at[2]),
    ]
    for copy in small:
        copy.start()
    pieces = field_sems.shape[0]
    bounds = [levels * i // pieces for i in range(pieces + 1)]
    fields = []
    for i in range(pieces):
        part = pl.ds(bounds[i], bounds[i + 1] - bounds[i])
        pair = [
            pltpu.make_async_copy(u_hbm.at[0, part], u_ref.at[0, part], field_sems.at[i, 0]),
            pltpu.make_async_copy(k_hbm.at[0, part], k_ref.at[0, part], field_sems.at[i, 1]),
        ]
        for copy in pair:
            copy.start()
        fields.append(pair)
    blank = jnp.zeros((nx + 2 * SUB, LANES), F32)
    for t in range(tiles + 1):
        for ext in (ext_u, ext_k):
            ext[0, t] = blank
            ext[levels + 1, t] = blank
    for copy in small:
        copy.wait()
    for x in range(0, nx, SUB):
        rows = slice(x, x + SUB)
        kinds = kind_ref[0, rows]
        tables = [lambda p, l=l: lw[l, comp, p] for l in range(NS)]
        tables += [lambda p, l=l: lw[l, 1 - comp, p] for l in range(NS)]
        tables += [lambda p, q=q: table[q, p] for q in range(2)]
        found = [jnp.full(kinds.shape, t(0), F32) for t in tables]
        for p in range(1, PLANTS):
            here = kinds == p
            found = [jnp.where(here, t(p), f) for t, f in zip(tables, found)]
        for i, f in enumerate(found):
            prof[i, rows] = f

    for i in range(pieces):
        for copy in fields[i]:
            copy.wait()

        def level(l, _):
            for t in range(tiles):
                u = u_ref[0, l, :, t * LANES : (t + 1) * LANES]
                k = k_ref[0, l, :, t * LANES : (t + 1) * LANES]
                ext_u[l + 1, t, SUB : SUB + nx] = u
                ext_k[l + 1, t, SUB : SUB + nx] = k * (0.5 + 0.25 * jnp.tanh(u))
            return 0

        lax.fori_loop(bounds[i], bounds[i + 1], level, 0, unroll=2)
    force = prof[0] * u_ref[0, 0]
    for l in range(1, NS):
        force = force + prof[l] * u_ref[0, l]
    prof[2 * NS + 2] = force


def split(v):
    hi = v.astype(jnp.bfloat16)
    lo = (v - hi.astype(F32)).astype(jnp.bfloat16)
    return hi, lo


def source_kernel(rows_ref, part_ref, w_ref, prof, surf_ref, flux_ref, src_ref, out0, out1, picked):
    _, nx, ny = part_ref.shape
    first = lax.axis_index("comp") == 0
    odd = lax.axis_index("gx") % 2 == 1
    for x in range(nx):
        r = rows_ref[0, x]
        picked[:, pl.ds(x, 1), :] = part_ref[:, pl.ds(r, 1), :]
    forces = []
    for b in range(ny // PATCH):
        cols = slice(b * PATCH, (b + 1) * PATCH)
        x_hi, x_lo = split(picked[:, :, cols].reshape(NS * nx, PATCH))
        w_hi, w_lo = split(w_ref[0, cols, :])
        dims = (((1,), (1,)), ((), ()))
        y = lax.dot_general(x_hi, w_lo, dims, preferred_element_type=F32)
        y = y + lax.dot_general(x_lo, w_hi, dims, preferred_element_type=F32)
        y = y + lax.dot_general(x_hi, w_hi, dims, preferred_element_type=F32)
        y = y.reshape(NS, nx, PATCH)
        total = prof[NS, :, cols] * y[0]
        for l in range(1, NS):
            total = total + prof[NS + l, :, cols] * y[l]
        forces.append(total)
    other_force = jnp.concatenate(forces, axis=1)
    own_force = prof[2 * NS + 2]
    atmos = jnp.where(first, own_force, other_force)
    soil = jnp.where(first, other_force, own_force)
    flux = prof[2 * NS] * (prof[2 * NS + 1] * soil - atmos)
    flux_ref[0] = flux
    signed = jnp.where(first, flux, -flux)
    upper = iota((SUB, ny), 0) < HALO
    src = []
    for l in range(NS):
        s = signed * prof[l]
        if l == 0:
            s = s + surf_ref[0]
        src_ref[l] = s
        src.append(s)
    for j in range(NS // 2):
        a, b = src[2 * j], src[2 * j + 1]
        low = jnp.where(upper, a[:SUB], half_swap(b[:SUB]))
        high = jnp.where(upper, half_swap(a[nx - SUB :]), b[nx - SUB :])
        out0[j] = jnp.where(odd, low, high)
        out1[j] = jnp.where(odd, high, low)


def columns_kernel(start, ext_u_in, ext_k_in, s_ref, x0, x1, s0, s1, ext_u, ext_k, ext_s, out0, out1):
    levels = ext_u.shape[0] - 2
    nx, ny = s_ref.shape[1:]
    tiles = ny // LANES
    upper = iota((SUB, LANES), 0) < HALO
    gx, count = lax.axis_index("gx"), lax.axis_size("gx")
    odd = gx % 2 == 1
    keep_low = upper & (gx < 0) | ~upper & (gx > 0)
    keep_high = upper & (gx < count - 1)

    def halves(first, second, j, cols):
        a, b = first[j, :, cols], second[j, :, cols]
        high, low = jnp.where(odd, b, a), jnp.where(odd, a, b)
        lows = jnp.where(keep_low, half_swap(low), 0.0), jnp.where(keep_low, low, 0.0)
        highs = jnp.where(keep_high, high, 0.0), jnp.where(keep_high, half_swap(high), 0.0)
        return lows, highs

    def level(l, _):
        for t in range(tiles):
            lows, highs = halves(x0, x1, l, slice(t * LANES, (t + 1) * LANES))
            for rows, (u, k) in ((slice(0, SUB), lows), (slice(SUB + nx, 2 * SUB + nx), highs)):
                ext_u[l + 1, t, rows] = u
                ext_k[l + 1, t, rows] = k * (0.5 + 0.25 * jnp.tanh(u))
        return 0

    lax.fori_loop(0, levels, level, 0, unroll=2)
    for j in range(NS // 2):
        for t in range(tiles):
            cols = slice(t * LANES, (t + 1) * LANES)
            lows, highs = halves(s0, s1, j, cols)
            for i in range(2):
                ext_s[2 * j + i, t, :SUB] = lows[i]
                ext_s[2 * j + i, t, SUB : SUB + nx] = s_ref[2 * j + i, :, cols]
                ext_s[2 * j + i, t, SUB + nx :] = highs[i]

    y_odd = lax.axis_index("gy") % 2
    window = nx + 2 * HALO
    group = iota((window, LANES), 1) // HALO
    first_high = y_odd == 0
    tile0 = jnp.where(first_high, tiles - 1, 0)
    tile1 = tiles - 1 - tile0
    move0 = jnp.where(first_high, HALO, 0)
    move1 = HALO - move0
    for f, (ext, base, n) in enumerate(((ext_u, 1, levels), (ext_k, 1, levels), (ext_s, 0, NS))):
        for out, tile, move in ((out0, tile0, move0), (out1, tile1, move1)):
            packed = jnp.zeros((window, LANES), F32)
            for l in range(n):
                v = ext[l + base, tile, pl.ds(start[0], window)]
                v = pltpu.roll(v, (HALO * l + move) % LANES, 1)
                packed = jnp.where(group == l, v, packed)
            out[f] = packed


def chain_kernel(
    start, storage_ref, ext_u_in, ext_k_in, ext_s, y0, y1, flux,
    ext_u, r, p1, p2, moments, flux_out,
    cz, cx, cy, cy_low, diag, inside, sem,
):
    flux_copy = pltpu.make_async_copy(flux, flux_out, sem)
    flux_copy.start()
    levels = ext_u.shape[0] - 2
    tiles, all_rows = ext_u.shape[1] - 1, ext_u.shape[2]
    nx = all_rows - 2 * SUB
    window = nx + 2 * HALO
    gx, gy, ngx, ngy = lax.axis_index("gx"), lax.axis_index("gy"), lax.axis_size("gx"), lax.axis_size("gy")
    odd = gy % 2 == 1
    has_low, has_high = gy > 0, gy < ngy - 1
    lane = iota((window, LANES), 1)
    keep_high = lane < jnp.where(has_high, HALO, 0)
    keep_low = lane >= jnp.where(has_low, LANES - HALO, LANES)
    base = start[0]
    ext_k = ext_k_in

    def third(f, l):
        a, b = y0[f], y1[f]
        high, low = jnp.where(odd, b, a), jnp.where(odd, a, b)
        high = pltpu.roll(high, (LANES - HALO * l) % LANES, 1) if (HALO * l) % LANES else high
        low = pltpu.roll(low, (2 * LANES - HALO - HALO * l) % LANES, 1)
        return jnp.where(keep_high, high, jnp.where(keep_low, low, 0.0))

    zero_tile = jnp.zeros((SUB, LANES), F32)
    for l in range(levels):
        for f, ext in enumerate((ext_u, ext_k)):
            ext[l + 1, tiles, :SUB] = zero_tile
            ext[l + 1, tiles, SUB + nx :] = zero_tile
            ext[l + 1, tiles, pl.ds(base, window)] = third(f, l)
    blank = jnp.zeros((all_rows, LANES), F32)
    for t in range(tiles + 1):
        for ext in (r, p1, p2):
            ext[0, t] = blank
            ext[levels + 1, t] = blank

    row = iota((all_rows, LANES), 0) - SUB
    col = iota((all_rows, LANES), 1)
    row_ok = ((row >= 0) & (row < nx)) | ((row >= nx) & (gx < ngx - 1)) | ((row < 0) & (gx > 0))
    col_ok = ((col < HALO) & has_high) | ((col >= LANES - HALO) & has_low)
    inside[0] = jnp.where(row_ok, 1.0, 0.0)
    inside[1] = jnp.where(row_ok & col_ok, 1.0, 0.0)

    lane8 = iota((SUB, LANES), 1)
    at_end, at_start = lane8 == LANES - 1, lane8 == 0

    def beside(vs):
        n = len(vs)
        up = [pltpu.roll(v, LANES - 1, 1) for v in vs]
        down = [pltpu.roll(v, 1, 1) for v in vs]
        ups = [jnp.where(at_end, up[(t + 1) % n], up[t]) for t in range(n)]
        downs = [jnp.where(at_start, down[(t - 1) % n], down[t]) for t in range(n)]
        return ups, downs

    def masked(w, t, at, chunk):
        if t == tiles:
            return w * inside[1, pl.ds(at, SUB)]
        if chunk in (0, chunks - 1):
            return w * inside[0, pl.ds(at, SUB)]
        return w

    shift = storage_ref[0] - CENTRE
    chunks = window // SUB
    every = range(tiles + 1)
    few = next(n for n in (3, 2, 1) if levels % n == 0)
    many = next(n for n in (6, 5, 4, 3, 2, 1) if levels % n == 0)

    def prepare(j, _):
        first = j * few
        for c in range(chunks):
            at = base + SUB * c
            rows = pl.ds(at, SUB)

            def load(ext, plane, dx=0):
                return [ext[first + plane, t, pl.ds(at + dx, SUB)] for t in every]

            k_last, u_last = load(ext_k, 0), load(ext_u, 0)
            k, u = load(ext_k, 1), load(ext_u, 1)
            below = [k[t] + k_last[t] for t in every]
            for i in range(few):
                l = first + i
                k_next, u_next = load(ext_k, i + 2), load(ext_u, i + 2)
                ks = [load(ext_k, i + 1, dx) for dx in (1, -1)]
                us = [load(ext_u, i + 1, dx) for dx in (1, -1)]
                yk, yu = beside(k), beside(u)
                above = [k[t] + k_next[t] for t in every]
                for t in every:
                    y_up, y_down = yk[0][t] + k[t], yk[1][t] + k[t]
                    x_up, x_down = ks[0][t] + k[t], ks[1][t] + k[t]
                    total = ((y_up + y_down) + (x_up + x_down)) + (above[t] + below[t])
                    flow = (y_up * yu[0][t] + y_down * yu[1][t]) + (x_up * us[0][t] + x_down * us[1][t])
                    flow = flow + (above[t] * u_next[t] + below[t] * u_last[t])
                    cy[l, t, rows] = y_up
                    cy_low[l, t, rows] = y_down
                    cx[l, t, rows] = x_up
                    cz[l, t, rows] = below[t]
                    diag[l, t, rows] = total + shift
                    r[l + 1, t, rows] = masked(flow - total * u[t], t, at, c)
                k_last, u_last, k, u, below = k, u, k_next, u_next, above
        return 0

    lax.fori_loop(0, levels // few, prepare, 0)
    for c in range(chunks):
        at = base + SUB * c
        for t in every:
            cz[levels, t, pl.ds(at, SUB)] = zero_tile
    for l in range(NS):
        for t in range(tiles):
            rows = pl.ds(base, window)
            r[l + 1, t, rows] = r[l + 1, t, rows] + ext_s[l, t, rows]
        rows = pl.ds(base, window)
        r[l + 1, tiles, rows] = r[l + 1, tiles, rows] + third(2, l)

    def operator(src, l, at, outs, unroll):
        rows = pl.ds(at, SUB)
        planes = [[src[l + i, t, rows] for t in every] for i in range(unroll + 2)]
        faces = [[cz[l + i, t, rows] for t in outs] for i in range(unroll + 1)]
        for i in range(unroll):
            v = planes[i + 1]
            v_up, v_down = beside(v)
            ws = []
            for t in outs:
                z = faces[i + 1][t] * planes[i + 2][t] + faces[i][t] * planes[i][t]
                x = cx[l + i, t, rows] * src[l + i + 1, t, pl.ds(at + 1, SUB)]
                x = x + cx[l + i, t, pl.ds(at - 1, SUB)] * src[l + i + 1, t, pl.ds(at - 1, SUB)]
                y = cy[l + i, t, rows] * v_up[t] + cy_low[l + i, t, rows] * v_down[t]
                ws.append((diag[l + i, t, rows] * v[t] - z) - (x + y))
            yield i, v, ws

    def apply(src, dst):
        def step(j, _):
            l = j * many
            for c in range(chunks):
                at = base + SUB * c
                for i, _, ws in operator(src, l, at, every, many):
                    for t, w in enumerate(ws):
                        dst[l + i + 1, t, pl.ds(at, SUB)] = masked(w, t, at, c)
            return 0

        lax.fori_loop(0, levels // many, step, 0)

    apply(r, p1)
    apply(p1, p2)

    def last(j, sums):
        l = j * many
        sums = list(sums)
        for c in range(nx // SUB):
            at = SUB + SUB * c
            for i, v, ws in operator(p2, l, at, range(tiles), many):
                for t in range(tiles):
                    rows = pl.ds(at, SUB)
                    a, b, w = r[l + i + 1, t, rows], p1[l + i + 1, t, rows], ws[t]
                    for q, term in enumerate((a * a, a * b, b * b, b * v[t], v[t] * v[t], v[t] * w, w * w)):
                        sums[q] = sums[q] + term
        return tuple(sums)

    sums = lax.fori_loop(0, levels // many, last, (zero_tile,) * MOMENTS)
    which = iota((SUB, LANES), 0)
    packed = zero_tile
    for i, m in enumerate(sums):
        total = jnp.sum(jnp.sum(m, axis=1, keepdims=True), axis=0, keepdims=True)
        packed = jnp.where(which == i, total, packed)
    moments[...] = packed
    flux_copy.wait()


def add_kernel(*refs):
    *ins, out = refs
    total = ins[0][...]
    for x in ins[1:]:
        total = total + x[...]
    out[...] = total


def update_kernel(*refs):
    *parts, u_ref, r, p1, p2, out, stage, sems = refs
    total = parts[0][...]
    for x in parts[1:]:
        total = total + x[...]
    m = [total[i : i + 1, :] for i in range(MOMENTS)]

    def gram(i, j):
        return m[i + j + 2] + 2.0 * CENTRE * m[i + j + 1] + CENTRE * CENTRE * m[i + j]

    b = [m[i + 1] + CENTRE * m[i] for i in range(ITERS)]
    l00 = jnp.sqrt(gram(0, 0))
    l10 = gram(1, 0) / l00
    l20 = gram(2, 0) / l00
    l11 = jnp.sqrt(gram(1, 1) - l10 * l10)
    l21 = (gram(2, 1) - l20 * l10) / l11
    l22 = jnp.sqrt(gram(2, 2) - l20 * l20 - l21 * l21)
    z0 = b[0] / l00
    z1 = (b[1] - l10 * z0) / l11
    z2 = (b[2] - l20 * z0 - l21 * z1) / l22
    c2 = z2 / l22
    c1 = (z1 - l21 * c2) / l11
    c0 = (z0 - l10 * c1 - l20 * c2) / l00
    _, levels, nx, ny = stage.shape
    c0, c1, c2 = (jnp.broadcast_to(c, (nx, LANES)) for c in (c0, c1, c2))
    pieces = sems.shape[0]
    per = levels // pieces
    copies = []
    for piece in range(pieces):
        lo = piece * per
        n = per if piece < pieces - 1 else levels - lo

        def step(l, _):
            for t in range(ny // LANES):
                rows = slice(SUB, SUB + nx)
                v = u_ref[l + 1, t, rows] + c0 * r[l + 1, t, rows]
                v = v + (c1 * p1[l + 1, t, rows] + c2 * p2[l + 1, t, rows])
                stage[0, l, :, t * LANES : (t + 1) * LANES] = v
            return 0

        lax.fori_loop(lo, lo + n, step, 0, unroll=2)
        copy = pltpu.make_async_copy(stage.at[0, pl.ds(lo, n)], out.at[0, pl.ds(lo, n)], sems.at[piece])
        copy.start()
        copies.append(copy)
    for copy in copies:
        copy.wait()


def body(
    state, conduct, storage, surface_source, plant_type, plant_table, layer_weights, remap_rows, remap_weights
):
    levels, nx, ny = state.shape[1:]
    tiles = ny // LANES
    window = nx + 2 * HALO
    start = jnp.full((1,), SUB - HALO, jnp.int32)
    edge = pltpu.VMEM((levels, SUB, ny), F32)
    (layers,) = call(
        layers_kernel, [(NS, nx, ny)], [state], "layers", scratch=[pltpu.SemaphoreType.DMA(())], hbm=(0,)
    )
    partner = lax.ppermute(layers, "comp", [(i, i ^ 1) for i in range(lax.axis_size("comp"))])
    x0, x1 = call(
        edges_kernel,
        [(levels, SUB, ny)] * 2,
        [state, conduct],
        "edges",
        scratch=[edge] * 4 + [pltpu.SemaphoreType.DMA((4,))],
        hbm=(0, 1),
    )
    x0, x1 = swap(x0, "gx", 0), swap(x1, "gx", 1)
    ext = (levels + 2, tiles + 1, nx + 2 * SUB, LANES)
    ext_s = (NS, tiles, nx + 2 * SUB, LANES)
    table, weights = plant_table.T, layer_weights.transpose(2, 0, 1)
    ext_u, ext_k, prof = call(
        own_kernel,
        [ext, ext, (PROFILES, nx, ny)],
        [table, weights, state, conduct, plant_type],
        "own",
        scratch=[
            pltpu.SMEM(table.shape, F32),
            pltpu.SMEM(weights.shape, F32),
            pltpu.VMEM(state.shape, F32),
            pltpu.VMEM(state.shape, F32),
            pltpu.VMEM(plant_type.shape, jnp.int32),
            pltpu.SemaphoreType.DMA((3,)),
            pltpu.SemaphoreType.DMA((3, 2)),
        ],
        hbm=(0, 1, 2, 3, 4),
        limit=4,
    )
    flux, src, s0, s1 = call(
        source_kernel,
        [(1, nx, ny), (NS, nx, ny)] + [(NS // 2, SUB, ny)] * 2,
        [remap_rows, partner, remap_weights, prof, surface_source],
        "source",
        scratch=[pltpu.VMEM((NS, nx, ny), F32)],
        smem=(0,),
    )
    s0, s1 = swap(s0, "gx", 0), swap(s1, "gx", 1)
    ext_u, ext_k, ext_s, y0, y1 = call(
        columns_kernel,
        [ext, ext, ext_s] + [(3, window, LANES)] * 2,
        [start, ext_u, ext_k, src, x0, x1, s0, s1],
        "columns",
        smem=(0,),
        alias={1: 0, 2: 1},
    )
    y0, y1 = swap(y0, "gy", 0), swap(y1, "gy", 1)
    coef = pltpu.VMEM((levels,) + ext[1:], F32)
    ext_u, r, p1, p2, moments, flux = call(
        chain_kernel,
        [ext] * 4 + [(SUB, LANES), (1, nx, ny)],
        [start, storage, ext_u, ext_k, ext_s, y0, y1, flux],
        "chain",
        scratch=[pltpu.VMEM((levels + 1,) + ext[1:], F32)]
        + [coef] * 4
        + [pltpu.VMEM((2, nx + 2 * SUB, LANES), F32), pltpu.SemaphoreType.DMA(())],
        hbm_outs=(5,),
        smem=(0, 1),
        limit=16,
        alias={2: 0},
    )
    (moments,) = call(add_kernel, [(SUB, LANES)], everyone(moments, "gx"), "add")
    parts = everyone(moments, "gy")
    (new_state,) = call(
        update_kernel,
        [state.shape],
        parts + [ext_u, r, p1, p2],
        "update",
        scratch=[pltpu.VMEM(state.shape, F32), pltpu.SemaphoreType.DMA((3,))],
        hbm_outs=(0,),
    )
    return new_state, flux


def solution(mesh):
    in_specs = (
        P("comp", None, "gx", "gy"),
        P("comp", None, "gx", "gy"),
        P("comp"),
        P("comp", "gx", "gy"),
        P("comp", "gx", "gy"),
        P(),
        P(),
        P("comp", "gx"),
        P("comp", "gy", None),
    )
    out_specs = (P("comp", None, "gx", "gy"), P("comp", "gx", "gy"))
    return jax.shard_map(body, mesh=mesh, in_specs=in_specs, out_specs=out_specs, check_vma=False)
```

```python
import jax
import jax.numpy as jnp
from jax import lax
from jax.experimental import pallas as pl
from jax.experimental.pallas import tpu as pltpu
from jax.sharding import PartitionSpec as P

NS = 6
PATCH = 128
PLANTS = 16
ITERS = 3
HALO = ITERS + 1
CENTRE = 8.0
LANES = 128
SUB = 8
MOMENTS = 2 * ITERS + 1
PROFILES = 2 * NS + 3
F32 = jnp.float32
MIB = 1 << 20


def swap(value, axis, which):
    nx, ny = lax.axis_size("gx"), lax.axis_size("gy")

    def partner(i, count):
        p = i ^ 1 if which == 0 else (i + 1 if i % 2 else i - 1)
        return p if 0 <= p < count else None

    def target(i, j):
        p = partner(i, nx) if axis == "gx" else partner(j, ny)
        if axis == "gx":
            i, j = (p, j) if p is not None else (i, j ^ 1 if ny % 2 == 0 else j)
        else:
            i, j = (i, p) if p is not None else (i ^ 1 if nx % 2 == 0 else i, j)
        return i * ny + j

    pairs = [(i * ny + j, target(i, j)) for i in range(nx) for j in range(ny)]
    return lax.ppermute(value, ("gx", "gy"), pairs)


def everyone(value, axis):
    n = lax.axis_size(axis)
    return [value] + [lax.ppermute(value, axis, [(i, i ^ d) for i in range(n)]) for d in range(1, n)]


def iota(shape, dim):
    return lax.broadcasted_iota(jnp.int32, shape, dim)


VMEM_SPEC = pl.BlockSpec(memory_space=pltpu.VMEM)
SMEM_SPEC = pl.BlockSpec(memory_space=pltpu.SMEM)
HBM_SPEC = pl.BlockSpec(memory_space=pltpu.HBM)


def call(kernel, outs, ins, scratch=(), smem=(), hbm=(), hbm_outs=(), limit=2, alias=None):
    def spec(i):
        return SMEM_SPEC if i in smem else HBM_SPEC if i in hbm else VMEM_SPEC

    def place(i, v):
        if i in smem:
            return v
        return pltpu.with_memory_space_constraint(v, pltpu.HBM if i in hbm else pltpu.VMEM)

    return pl.pallas_call(
        kernel,
        out_shape=[jax.ShapeDtypeStruct(s, F32) if i in hbm_outs else pltpu.VMEM(s, F32) for i, s in enumerate(outs)],
        in_specs=[spec(i) for i in range(len(ins))],
        out_specs=[HBM_SPEC if i in hbm_outs else VMEM_SPEC for i in range(len(outs))],
        scratch_shapes=list(scratch),
        input_output_aliases=alias or {},
        compiler_params=pltpu.CompilerParams(vmem_limit_bytes=limit * MIB),
    )(*[place(i, v) for i, v in enumerate(ins)])


def half_swap(v):
    return pltpu.roll(v, HALO, 0)


def layers_kernel(u_hbm, layers, sem):
    copy = pltpu.make_async_copy(u_hbm.at[0, pl.ds(0, NS)], layers, sem)
    copy.start()
    copy.wait()


def edges_kernel(after, u_hbm, k_hbm, out0, out1, low_u, low_k, high_u, high_k, sems):
    _, levels, rows, cols = u_hbm.shape
    copies = [
        pltpu.make_async_copy(u_hbm.at[0, :, pl.ds(0, SUB)], low_u, sems.at[0]),
        pltpu.make_async_copy(k_hbm.at[0, :, pl.ds(0, SUB)], low_k, sems.at[1]),
        pltpu.make_async_copy(u_hbm.at[0, :, pl.ds(rows - SUB, SUB)], high_u, sems.at[2]),
        pltpu.make_async_copy(k_hbm.at[0, :, pl.ds(rows - SUB, SUB)], high_k, sems.at[3]),
    ]
    for c in copies:
        c.start()
    upper = iota((SUB, cols), 0) < HALO
    odd = lax.axis_index("gx") % 2 == 1
    for c in copies:
        c.wait()
    for l in range(levels):
        low = jnp.where(upper, low_u[l], half_swap(low_k[l]))
        high = jnp.where(upper, half_swap(high_u[l]), high_k[l])
        out0[l] = jnp.where(odd, low, high)
        out1[l] = jnp.where(odd, high, low)


def profile_kernel(table_hbm, lw_hbm, kind_hbm, layers, prof, table, lw, kind_ref, sems):
    nx = layers.shape[1]
    comp = lax.axis_index("comp")
    copies = [
        pltpu.make_async_copy(table_hbm, table, sems.at[0]),
        pltpu.make_async_copy(lw_hbm, lw, sems.at[1]),
        pltpu.make_async_copy(kind_hbm, kind_ref, sems.at[2]),
    ]
    for copy in copies:
        copy.start()
    for copy in copies:
        copy.wait()
    for x in range(0, nx, SUB):
        rows = slice(x, x + SUB)
        kinds = kind_ref[0, rows]
        tables = [lambda p, l=l: lw[l, comp, p] for l in range(NS)]
        tables += [lambda p, l=l: lw[l, 1 - comp, p] for l in range(NS)]
        tables += [lambda p, q=q: table[q, p] for q in range(2)]
        found = [jnp.full(kinds.shape, t(0), F32) for t in tables]
        for p in range(1, PLANTS):
            here = kinds == p
            found = [jnp.where(here, t(p), f) for t, f in zip(tables, found)]
        force = found[0] * layers[0, rows]
        for l in range(1, NS):
            force = force + found[l] * layers[l, rows]
        for i, f in enumerate(found + [force]):
            prof[i, rows] = f


def received_rows(count):
    upper = iota((SUB, LANES), 0) < HALO
    gx = lax.axis_index("gx")
    odd = gx % 2 == 1
    keep_low = ~upper & (gx > 0)
    keep_high = upper & (gx < count - 1)

    def halves(first, second, j, cols):
        a, b = first[j, :, cols], second[j, :, cols]
        high, low = jnp.where(odd, b, a), jnp.where(odd, a, b)
        lows = jnp.where(keep_low, half_swap(low), 0.0), jnp.where(keep_low, low, 0.0)
        highs = jnp.where(keep_high, high, 0.0), jnp.where(keep_high, half_swap(high), 0.0)
        return lows, highs

    return halves


def pack_columns(ext, plane, count, base, window, tiles, outs, slot):
    group = iota((window, LANES), 1) // HALO
    first_high = lax.axis_index("gy") % 2 == 0
    tile0 = jnp.where(first_high, tiles - 1, 0)
    move0 = jnp.where(first_high, HALO, 0)
    for out, tile, move in ((outs[0], tile0, move0), (outs[1], tiles - 1 - tile0, HALO - move0)):
        packed = jnp.zeros((window, LANES), F32)
        for l in range(count):
            v = ext[l + plane, tile, pl.ds(base, window)]
            v = pltpu.roll(v, (HALO * l + move) % LANES, 1)
            packed = jnp.where(group == l, v, packed)
        out[slot] = packed


def fields_kernel(start, after, u_ref, k_ref, x0, x1, ext_u, ext_k, out0, out1):
    _, levels, nx, ny = u_ref.shape
    tiles = ny // LANES
    blank = jnp.zeros((nx + 2 * SUB, LANES), F32)
    for t in range(tiles + 1):
        for ext in (ext_u, ext_k):
            ext[0, t] = blank
            ext[levels + 1, t] = blank
    halves = received_rows(lax.axis_size("gx"))

    def level(l, _):
        for t in range(tiles):
            cols = slice(t * LANES, (t + 1) * LANES)
            lows, highs = halves(x0, x1, l, cols)
            own = u_ref[0, l, :, cols], k_ref[0, l, :, cols]
            for rows, (u, k) in (
                (slice(0, SUB), lows),
                (slice(SUB, SUB + nx), own),
                (slice(SUB + nx, 2 * SUB + nx), highs),
            ):
                ext_u[l + 1, t, rows] = u
                ext_k[l + 1, t, rows] = k * (0.5 + 0.25 * jnp.tanh(u))
        return 0

    lax.fori_loop(0, levels, level, 0, unroll=2)
    for slot, ext in enumerate((ext_u, ext_k)):
        pack_columns(ext, 1, levels, start[0], nx + 2 * HALO, tiles, (out0, out1), slot)


def split(v):
    hi = v.astype(jnp.bfloat16)
    lo = (v - hi.astype(F32)).astype(jnp.bfloat16)
    return hi, lo


def source_kernel(rows_ref, part_ref, w_ref, prof, surf_ref, flux_ref, src_ref, out0, out1, picked):
    _, nx, ny = part_ref.shape
    first = lax.axis_index("comp") == 0
    odd = lax.axis_index("gx") % 2 == 1
    for x in range(nx):
        r = rows_ref[0, x]
        picked[:, pl.ds(x, 1), :] = part_ref[:, pl.ds(r, 1), :]
    forces = []
    for b in range(ny // PATCH):
        cols = slice(b * PATCH, (b + 1) * PATCH)
        x_hi, x_lo = split(picked[:, :, cols].reshape(NS * nx, PATCH))
        w_hi, w_lo = split(w_ref[0, cols, :])
        dims = (((1,), (1,)), ((), ()))
        y = lax.dot_general(x_hi, w_lo, dims, preferred_element_type=F32)
        y = y + lax.dot_general(x_lo, w_hi, dims, preferred_element_type=F32)
        y = y + lax.dot_general(x_hi, w_hi, dims, preferred_element_type=F32)
        y = y.reshape(NS, nx, PATCH)
        total = prof[NS, :, cols] * y[0]
        for l in range(1, NS):
            total = total + prof[NS + l, :, cols] * y[l]
        forces.append(total)
    other_force = jnp.concatenate(forces, axis=1)
    own_force = prof[2 * NS + 2]
    atmos = jnp.where(first, own_force, other_force)
    soil = jnp.where(first, other_force, own_force)
    flux = prof[2 * NS] * (prof[2 * NS + 1] * soil - atmos)
    flux_ref[0] = flux
    signed = jnp.where(first, flux, -flux)
    upper = iota((SUB, ny), 0) < HALO
    src = []
    for l in range(NS):
        s = signed * prof[l]
        if l == 0:
            s = s + surf_ref[0]
        src_ref[l] = s
        src.append(s)
    for j in range(NS // 2):
        a, b = src[2 * j], src[2 * j + 1]
        low = jnp.where(upper, a[:SUB], half_swap(b[:SUB]))
        high = jnp.where(upper, half_swap(a[nx - SUB :]), b[nx - SUB :])
        out0[j] = jnp.where(odd, low, high)
        out1[j] = jnp.where(odd, high, low)


def columns_kernel(start, s_ref, s0, s1, in0, in1, ext_s, out0, out1):
    nx, ny = s_ref.shape[1:]
    tiles = ny // LANES
    halves = received_rows(lax.axis_size("gx"))
    for j in range(NS // 2):
        for t in range(tiles):
            cols = slice(t * LANES, (t + 1) * LANES)
            lows, highs = halves(s0, s1, j, cols)
            for i in range(2):
                ext_s[2 * j + i, t, :SUB] = lows[i]
                ext_s[2 * j + i, t, SUB : SUB + nx] = s_ref[2 * j + i, :, cols]
                ext_s[2 * j + i, t, SUB + nx :] = highs[i]
    pack_columns(ext_s, 0, NS, start[0], nx + 2 * HALO, tiles, (out0, out1), 2)


def coefficients_kernel(start, storage_ref, after, ext_u, ext_k, r, cz, cx, cy, cy_low, diag):
    levels = ext_u.shape[0] - 2
    tiles = ext_u.shape[1] - 1
    nx = ext_u.shape[2] - 2 * SUB
    gx, ngx = lax.axis_index("gx"), lax.axis_size("gx")
    base = start[0]
    shift = storage_ref[0] - CENTRE
    chunks = (nx + 2 * HALO) // SUB
    few = next(n for n in (3, 2, 1) if levels % n == 0)
    own = range(tiles)
    lane, row = iota((SUB, LANES), 1), iota((SUB, LANES), 0)
    at_end, at_start = lane == LANES - 1, lane == 0
    low_rows = (row >= HALO) | (gx > 0)
    high_rows = (row < HALO) | (gx < ngx - 1)

    def beside(vs):
        up = [pltpu.roll(v, LANES - 1, 1) for v in vs] + [0.0]
        down = [0.0] + [pltpu.roll(v, 1, 1) for v in vs]
        ups = [jnp.where(at_end, up[t + 1], up[t]) for t in own]
        downs = [jnp.where(at_start, down[t], down[t + 1]) for t in own]
        return ups, downs

    def prepare(j, _):
        first = j * few
        for c in range(chunks):
            at = base + SUB * c
            rows = pl.ds(at, SUB)

            def load(ext, plane, dx=0):
                return [ext[first + plane, t, pl.ds(at + dx, SUB)] for t in own]

            k_last, u_last = load(ext_k, 0), load(ext_u, 0)
            k, u = load(ext_k, 1), load(ext_u, 1)
            below = [k[t] + k_last[t] for t in own]
            for i in range(few):
                l = first + i
                k_next, u_next = load(ext_k, i + 2), load(ext_u, i + 2)
                ks = [load(ext_k, i + 1, dx) for dx in (1, -1)]
                us = [load(ext_u, i + 1, dx) for dx in (1, -1)]
                yk, yu = beside(k), beside(u)
                above = [k[t] + k_next[t] for t in own]
                for t in own:
                    y_up, y_down = yk[0][t] + k[t], yk[1][t] + k[t]
                    x_up, x_down = ks[0][t] + k[t], ks[1][t] + k[t]
                    total = ((y_up + y_down) + (x_up + x_down)) + (above[t] + below[t])
                    flow = (y_up * yu[0][t] + y_down * yu[1][t]) + (x_up * us[0][t] + x_down * us[1][t])
                    flow = flow + (above[t] * u_next[t] + below[t] * u_last[t])
                    flow = flow - total * u[t]
                    if c == 0:
                        flow = jnp.where(low_rows, flow, 0.0)
                    if c == chunks - 1:
                        flow = jnp.where(high_rows, flow, 0.0)
                    cy[l, t, rows] = y_up
                    cy_low[l, t, rows] = y_down
                    cx[l, t, rows] = x_up
                    cz[l, t, rows] = below[t]
                    diag[l, t, rows] = total + shift
                    r[l + 1, t, rows] = flow
                k_last, u_last, k, u, below = k, u, k_next, u_next, above
        return 0

    lax.fori_loop(0, levels // few, prepare, 0)


def chain_kernel(
    start, storage_ref, ext_u_in, ext_k, ext_s, y0, y1, flux, r_in, cz_in, cx_in, cy_in, cy_low_in, diag_in,
    ext_u, p1, p2, moments, flux_out, r, cz, cx, cy, cy_low, diag,
    inside, sem,
):
    flux_copy = pltpu.make_async_copy(flux, flux_out, sem)
    flux_copy.start()
    levels = ext_u.shape[0] - 2
    tiles, all_rows = ext_u.shape[1] - 1, ext_u.shape[2]
    nx = all_rows - 2 * SUB
    window = nx + 2 * HALO
    gx, gy, ngx, ngy = lax.axis_index("gx"), lax.axis_index("gy"), lax.axis_size("gx"), lax.axis_size("gy")
    odd = gy % 2 == 1
    has_low, has_high = gy > 0, gy < ngy - 1
    lane = iota((window, LANES), 1)
    keep_high = lane < jnp.where(has_high, HALO, 0)
    keep_low = lane >= jnp.where(has_low, LANES - HALO, LANES)
    base = start[0]

    def third(f, l):
        a, b = y0[f], y1[f]
        high, low = jnp.where(odd, b, a), jnp.where(odd, a, b)
        high = pltpu.roll(high, (LANES - HALO * l) % LANES, 1) if (HALO * l) % LANES else high
        low = pltpu.roll(low, (2 * LANES - HALO - HALO * l) % LANES, 1)
        return jnp.where(keep_high, high, jnp.where(keep_low, low, 0.0))

    zero_tile = jnp.zeros((SUB, LANES), F32)
    for l in range(levels):
        for f, ext in enumerate((ext_u, ext_k)):
            ext[l + 1, tiles, :SUB] = zero_tile
            ext[l + 1, tiles, SUB + nx :] = zero_tile
            ext[l + 1, tiles, pl.ds(base, window)] = third(f, l)
    blank = jnp.zeros((all_rows, LANES), F32)
    for t in range(tiles + 1):
        for ext in (r, p1, p2):
            ext[0, t] = blank
            ext[levels + 1, t] = blank

    row = iota((all_rows, LANES), 0) - SUB
    col = iota((all_rows, LANES), 1)
    row_ok = ((row >= 0) & (row < nx)) | ((row >= nx) & (gx < ngx - 1)) | ((row < 0) & (gx > 0))
    col_ok = ((col < HALO) & has_high) | ((col >= LANES - HALO) & has_low)
    inside[0] = jnp.where(row_ok, 1.0, 0.0)
    inside[1] = jnp.where(row_ok & col_ok, 1.0, 0.0)

    lane8 = iota((SUB, LANES), 1)
    at_end, at_start = lane8 == LANES - 1, lane8 == 0

    def beside(vs):
        n = len(vs)
        up = [pltpu.roll(v, LANES - 1, 1) for v in vs]
        down = [pltpu.roll(v, 1, 1) for v in vs]
        ups = [jnp.where(at_end, up[(t + 1) % n], up[t]) for t in range(n)]
        downs = [jnp.where(at_start, down[(t - 1) % n], down[t]) for t in range(n)]
        return ups, downs

    def masked(w, t, at, chunk):
        if t == tiles:
            return w * inside[1, pl.ds(at, SUB)]
        if chunk in (0, chunks - 1):
            return w * inside[0, pl.ds(at, SUB)]
        return w

    shift = storage_ref[0] - CENTRE
    chunks = window // SUB
    every = range(tiles + 1)
    few = next(n for n in (3, 2, 1) if levels % n == 0)
    many = next(n for n in (6, 5, 4, 3, 2, 1) if levels % n == 0)

    def prepare(j, _):
        first = j * few
        for c in range(chunks):
            at = base + SUB * c
            rows = pl.ds(at, SUB)

            def load(ext, plane, dx=0):
                return ext[first + plane, tiles, pl.ds(at + dx, SUB)]

            k_last, u_last = load(ext_k, 0), load(ext_u, 0)
            k, u = load(ext_k, 1), load(ext_u, 1)
            below = k + k_last
            for i in range(few):
                l = first + i
                k_next, u_next = load(ext_k, i + 2), load(ext_u, i + 2)
                edge = [[ext[l + 1, t, rows] for ext in (ext_k, ext_u)] for t in (0, tiles - 1)]
                k_up, u_up = pltpu.roll(k, LANES - 1, 1), pltpu.roll(u, LANES - 1, 1)
                k_down, u_down = pltpu.roll(k, 1, 1), pltpu.roll(u, 1, 1)
                ahead = [pltpu.roll(v, LANES - 1, 1) for v in edge[0]]
                behind = [pltpu.roll(v, 1, 1) for v in edge[1]]
                y_up = k + jnp.where(at_end, ahead[0], k_up)
                y_down = k + jnp.where(at_start, behind[0], k_down)
                x_up, x_down = k + load(ext_k, i + 1, 1), k + load(ext_k, i + 1, -1)
                above = k + k_next
                total = ((y_up + y_down) + (x_up + x_down)) + (above + below)
                flow = y_up * jnp.where(at_end, ahead[1], u_up) + y_down * jnp.where(at_start, behind[1], u_down)
                flow = flow + (x_up * load(ext_u, i + 1, 1) + x_down * load(ext_u, i + 1, -1))
                flow = flow + (above * u_next + below * u_last)
                cy[l, tiles, rows] = y_up
                cy_low[l, tiles, rows] = y_down
                cx[l, tiles, rows] = x_up
                cz[l, tiles, rows] = below
                diag[l, tiles, rows] = total + shift
                r[l + 1, tiles, rows] = masked(flow - total * u, tiles, at, c)
                for t, (ko, uo), here, kn, un, face in (
                    (0, edge[0], at_start, k_down, u_down, cy_low),
                    (tiles - 1, edge[1], at_end, k_up, u_up, cy),
                ):
                    kn, un = jnp.where(here, kn, 0.0), jnp.where(here, un, 0.0)
                    face[l, t, rows] = face[l, t, rows] + kn
                    diag[l, t, rows] = diag[l, t, rows] + kn
                    r[l + 1, t, rows] = r[l + 1, t, rows] + ((ko + kn) * un - kn * uo)
                k_last, u_last, k, u, below = k, u, k_next, u_next, above
        return 0

    lax.fori_loop(0, levels // few, prepare, 0)
    for c in range(chunks):
        at = base + SUB * c
        for t in every:
            cz[levels, t, pl.ds(at, SUB)] = zero_tile
    for l in range(NS):
        for t in range(tiles):
            rows = pl.ds(base, window)
            r[l + 1, t, rows] = r[l + 1, t, rows] + ext_s[l, t, rows]
        rows = pl.ds(base, window)
        r[l + 1, tiles, rows] = r[l + 1, tiles, rows] + third(2, l)

    def operator(src, l, at, outs, unroll):
        rows = pl.ds(at, SUB)
        planes = [[src[l + i, t, rows] for t in every] for i in range(unroll + 2)]
        faces = [[cz[l + i, t, rows] for t in outs] for i in range(unroll + 1)]
        for i in range(unroll):
            v = planes[i + 1]
            v_up, v_down = beside(v)
            ws = []
            for t in outs:
                z = faces[i + 1][t] * planes[i + 2][t] + faces[i][t] * planes[i][t]
                x = cx[l + i, t, rows] * src[l + i + 1, t, pl.ds(at + 1, SUB)]
                x = x + cx[l + i, t, pl.ds(at - 1, SUB)] * src[l + i + 1, t, pl.ds(at - 1, SUB)]
                y = cy[l + i, t, rows] * v_up[t] + cy_low[l + i, t, rows] * v_down[t]
                ws.append((diag[l + i, t, rows] * v[t] - z) - (x + y))
            yield i, v, ws

    def apply(src, dst):
        def step(j, _):
            l = j * many
            for c in range(chunks):
                at = base + SUB * c
                for i, _, ws in operator(src, l, at, every, many):
                    for t, w in enumerate(ws):
                        dst[l + i + 1, t, pl.ds(at, SUB)] = masked(w, t, at, c)
            return 0

        lax.fori_loop(0, levels // many, step, 0)

    apply(r, p1)
    apply(p1, p2)

    def last(j, sums):
        l = j * many
        sums = list(sums)
        for c in range(nx // SUB):
            at = SUB + SUB * c
            for i, v, ws in operator(p2, l, at, range(tiles), many):
                for t in range(tiles):
                    rows = pl.ds(at, SUB)
                    a, b, w = r[l + i + 1, t, rows], p1[l + i + 1, t, rows], ws[t]
                    for q, term in enumerate((a * a, a * b, b * b, b * v[t], v[t] * v[t], v[t] * w, w * w)):
                        sums[q] = sums[q] + term
        return tuple(sums)

    sums = lax.fori_loop(0, levels // many, last, (zero_tile,) * MOMENTS)
    which = iota((SUB, LANES), 0)
    packed = zero_tile
    for i, m in enumerate(sums):
        total = jnp.sum(jnp.sum(m, axis=1, keepdims=True), axis=0, keepdims=True)
        packed = jnp.where(which == i, total, packed)
    moments[...] = packed
    flux_copy.wait()


def add_kernel(*refs):
    *ins, out = refs
    total = ins[0][...]
    for x in ins[1:]:
        total = total + x[...]
    out[...] = total


def update_kernel(*refs):
    *parts, u_ref, r, p1, p2, out, stage, sems = refs
    total = parts[0][...]
    for x in parts[1:]:
        total = total + x[...]
    m = [total[i : i + 1, :] for i in range(MOMENTS)]

    def gram(i, j):
        return m[i + j + 2] + 2.0 * CENTRE * m[i + j + 1] + CENTRE * CENTRE * m[i + j]

    b = [m[i + 1] + CENTRE * m[i] for i in range(ITERS)]
    l00 = jnp.sqrt(gram(0, 0))
    l10 = gram(1, 0) / l00
    l20 = gram(2, 0) / l00
    l11 = jnp.sqrt(gram(1, 1) - l10 * l10)
    l21 = (gram(2, 1) - l20 * l10) / l11
    l22 = jnp.sqrt(gram(2, 2) - l20 * l20 - l21 * l21)
    z0 = b[0] / l00
    z1 = (b[1] - l10 * z0) / l11
    z2 = (b[2] - l20 * z0 - l21 * z1) / l22
    c2 = z2 / l22
    c1 = (z1 - l21 * c2) / l11
    c0 = (z0 - l10 * c1 - l20 * c2) / l00
    _, levels, nx, ny = stage.shape
    c0, c1, c2 = (jnp.broadcast_to(c, (nx, LANES)) for c in (c0, c1, c2))
    pieces = sems.shape[0]
    per = levels // pieces
    copies = []
    for piece in range(pieces):
        lo = piece * per
        n = per if piece < pieces - 1 else levels - lo

        def step(l, _):
            for t in range(ny // LANES):
                rows = slice(SUB, SUB + nx)
                v = u_ref[l + 1, t, rows] + c0 * r[l + 1, t, rows]
                v = v + (c1 * p1[l + 1, t, rows] + c2 * p2[l + 1, t, rows])
                stage[0, l, :, t * LANES : (t + 1) * LANES] = v
            return 0

        lax.fori_loop(lo, lo + n, step, 0, unroll=2)
        copy = pltpu.make_async_copy(stage.at[0, pl.ds(lo, n)], out.at[0, pl.ds(lo, n)], sems.at[piece])
        copy.start()
        copies.append(copy)
    for copy in copies:
        copy.wait()


def step(
    state, conduct, storage, surface_source, plant_type, plant_table, layer_weights, remap_rows, remap_weights
):
    levels, nx, ny = state.shape[1:]
    tiles = ny // LANES
    window = nx + 2 * HALO
    start = jnp.full((1,), SUB - HALO, jnp.int32)
    edge = pltpu.VMEM((levels, SUB, ny), F32)
    (layers,) = call(layers_kernel, [(NS, nx, ny)], [state], scratch=[pltpu.SemaphoreType.DMA(())], hbm=(0,))
    partner = lax.ppermute(layers, "comp", [(i, i ^ 1) for i in range(lax.axis_size("comp"))])
    x0, x1 = call(
        edges_kernel,
        [(levels, SUB, ny)] * 2,
        [layers, state, conduct],
        scratch=[edge] * 4 + [pltpu.SemaphoreType.DMA((4,))],
        hbm=(1, 2),
    )
    x0, x1 = swap(x0, "gx", 0), swap(x1, "gx", 1)
    table, weights = plant_table.T, layer_weights.transpose(2, 0, 1)
    (prof,) = call(
        profile_kernel,
        [(PROFILES, nx, ny)],
        [table, weights, plant_type, layers],
        scratch=[
            pltpu.SMEM(table.shape, F32),
            pltpu.SMEM(weights.shape, F32),
            pltpu.VMEM(plant_type.shape, jnp.int32),
            pltpu.SemaphoreType.DMA((3,)),
        ],
        hbm=(0, 1, 2),
    )
    flux, src, s0, s1 = call(
        source_kernel,
        [(1, nx, ny), (NS, nx, ny)] + [(NS // 2, SUB, ny)] * 2,
        [remap_rows, partner, remap_weights, prof, surface_source],
        scratch=[pltpu.VMEM((NS, nx, ny), F32)],
        smem=(0,),
    )
    s0, s1 = swap(s0, "gx", 0), swap(s1, "gx", 1)
    ext = (levels + 2, tiles + 1, nx + 2 * SUB, LANES)
    ext_u, ext_k, y0, y1 = call(
        fields_kernel, [ext, ext] + [(3, window, LANES)] * 2, [start, src, state, conduct, x0, x1], smem=(0,)
    )
    ext_s, y0, y1 = call(
        columns_kernel,
        [(NS, tiles, nx + 2 * SUB, LANES)] + [(3, window, LANES)] * 2,
        [start, src, s0, s1, y0, y1],
        smem=(0,),
        alias={4: 1, 5: 2},
    )
    coef = (levels,) + ext[1:]
    coefs = call(
        coefficients_kernel,
        [ext, (levels + 1,) + ext[1:]] + [coef] * 4,
        [start, storage, ext_s, ext_u, ext_k],
        smem=(0, 1),
    )
    y0, y1 = swap(y0, "gy", 0), swap(y1, "gy", 1)
    ext_u, p1, p2, moments, flux, r, *_ = call(
        chain_kernel,
        [ext] * 3 + [(SUB, LANES), (1, nx, ny)] + [c.shape for c in coefs],
        [start, storage, ext_u, ext_k, ext_s, y0, y1, flux, *coefs],
        scratch=[pltpu.VMEM((2, nx + 2 * SUB, LANES), F32), pltpu.SemaphoreType.DMA(())],
        hbm_outs=(4,),
        smem=(0, 1),
        alias={2: 0, **{8 + i: 5 + i for i in range(len(coefs))}},
    )
    (moments,) = call(add_kernel, [(SUB, LANES)], everyone(moments, "gx"))
    parts = everyone(moments, "gy")
    (new_state,) = call(
        update_kernel,
        [state.shape],
        parts + [ext_u, r, p1, p2],
        scratch=[pltpu.VMEM(state.shape, F32), pltpu.SemaphoreType.DMA((3,))],
        hbm_outs=(0,),
    )
    return new_state, flux


def solution(mesh):
    in_specs = (
        P("comp", None, "gx", "gy"),
        P("comp", None, "gx", "gy"),
        P("comp"),
        P("comp", "gx", "gy"),
        P("comp", "gx", "gy"),
        P(),
        P(),
        P("comp", "gx"),
        P("comp", "gy", None),
    )
    out_specs = (P("comp", None, "gx", "gy"), P("comp", "gx", "gy"))
    return jax.shard_map(step, mesh=mesh, in_specs=in_specs, out_specs=out_specs, check_vma=False)
```

```python
import functools

import jax
import jax.numpy as jnp
from jax import lax
from jax.experimental import pallas as pl
from jax.experimental.pallas import tpu as pltpu
from jax.sharding import PartitionSpec as P

NS = 6
PATCH = 128
PLANTS = 16
ITERS = 3
HALO = ITERS + 1
CENTRE = 8.0
LANES = 128
SUB = 8
MOMENTS = 2 * ITERS + 1
PROFILES = 2 * NS + 3
F32 = jnp.float32
MIB = 1 << 20
EARLY = (2, 5)


def store(ext, plane, t, chunk, chunks, value):
    at = SUB + SUB * chunk
    ext[plane, t, at : at + SUB] = value
    if chunk == chunks - 1:
        ext[plane, t, :SUB] = value
    if chunk == 0:
        ext[plane, t, SUB + SUB * chunks :] = value


def swap(value, axis, which):
    nx, ny = lax.axis_size("gx"), lax.axis_size("gy")

    def partner(i, count):
        p = i ^ 1 if which == 0 else (i + 1 if i % 2 else i - 1)
        return p if 0 <= p < count else None

    def target(i, j):
        p = partner(i, nx) if axis == "gx" else partner(j, ny)
        if axis == "gx":
            i, j = (p, j) if p is not None else (i, j ^ 1 if ny % 2 == 0 else j)
        else:
            i, j = (i, p) if p is not None else (i ^ 1 if nx % 2 == 0 else i, j)
        return i * ny + j

    pairs = [(i * ny + j, target(i, j)) for i in range(nx) for j in range(ny)]
    return lax.ppermute(value, ("gx", "gy"), pairs)


def everyone(value, axis):
    n = lax.axis_size(axis)
    return [value] + [lax.ppermute(value, axis, [(i, i ^ d) for i in range(n)]) for d in range(1, n)]


def steps(levels, most):
    return max(n for n in range(1, most + 1) if levels % n == 0)


def iota(shape, dim):
    return lax.broadcasted_iota(jnp.int32, shape, dim)


VMEM_SPEC = pl.BlockSpec(memory_space=pltpu.VMEM)
SMEM_SPEC = pl.BlockSpec(memory_space=pltpu.SMEM)
HBM_SPEC = pl.BlockSpec(memory_space=pltpu.HBM)


def call(kernel, outs, ins, scratch=(), smem=(), hbm=(), hbm_outs=(), limit=2, alias=None):
    def spec(i):
        return SMEM_SPEC if i in smem else HBM_SPEC if i in hbm else VMEM_SPEC

    def place(i, v):
        if i in smem:
            return v
        return pltpu.with_memory_space_constraint(v, pltpu.HBM if i in hbm else pltpu.VMEM)

    return pl.pallas_call(
        kernel,
        out_shape=[jax.ShapeDtypeStruct(s, F32) if i in hbm_outs else pltpu.VMEM(s, F32) for i, s in enumerate(outs)],
        in_specs=[spec(i) for i in range(len(ins))],
        out_specs=[HBM_SPEC if i in hbm_outs else VMEM_SPEC for i in range(len(outs))],
        scratch_shapes=list(scratch),
        input_output_aliases=alias or {},
        compiler_params=pltpu.CompilerParams(vmem_limit_bytes=limit * MIB),
    )(*[place(i, v) for i, v in enumerate(ins)])


def half_swap(v):
    return pltpu.roll(v, HALO, 0)


def layers_kernel(u_hbm, layers, sem):
    copy = pltpu.make_async_copy(u_hbm.at[0, pl.ds(0, NS)], layers, sem)
    copy.start()
    copy.wait()


def edges_kernel(after, u_hbm, k_hbm, out0, out1, low_u, low_k, high_u, high_k, sems):
    _, levels, rows, cols = u_hbm.shape
    copies = [
        pltpu.make_async_copy(u_hbm.at[0, :, pl.ds(0, SUB)], low_u, sems.at[0]),
        pltpu.make_async_copy(k_hbm.at[0, :, pl.ds(0, SUB)], low_k, sems.at[1]),
        pltpu.make_async_copy(u_hbm.at[0, :, pl.ds(rows - SUB, SUB)], high_u, sems.at[2]),
        pltpu.make_async_copy(k_hbm.at[0, :, pl.ds(rows - SUB, SUB)], high_k, sems.at[3]),
    ]
    for c in copies:
        c.start()
    upper = iota((SUB, cols), 0) < HALO
    odd = lax.axis_index("gx") % 2 == 1
    for c in copies:
        c.wait()
    for l in range(levels):
        low = jnp.where(upper, low_u[l], half_swap(low_k[l]))
        high = jnp.where(upper, half_swap(high_u[l]), high_k[l])
        out0[l] = jnp.where(odd, low, high)
        out1[l] = jnp.where(odd, high, low)


def profile_kernel(
    table_hbm, lw_hbm, kind_hbm, layers, prof, table, lw, kind_ref, sems
):
    nx = layers.shape[1]
    comp = lax.axis_index("comp")
    copies = [
        pltpu.make_async_copy(table_hbm, table, sems.at[0]),
        pltpu.make_async_copy(lw_hbm, lw, sems.at[1]),
        pltpu.make_async_copy(kind_hbm, kind_ref, sems.at[2]),
    ]
    for copy in copies:
        copy.start()
    for copy in copies:
        copy.wait()
    for x in range(0, nx, SUB):
        rows = slice(x, x + SUB)
        kinds = kind_ref[0, rows]
        tables = [lambda p, l=l: lw[l, comp, p] for l in range(NS)]
        tables += [lambda p, l=l: lw[l, 1 - comp, p] for l in range(NS)]
        tables += [lambda p, q=q: table[q, p] for q in range(2)]
        found = [jnp.full(kinds.shape, t(0), F32) for t in tables]
        for p in range(1, PLANTS):
            here = kinds == p
            found = [jnp.where(here, t(p), f) for t, f in zip(tables, found)]
        force = found[0] * layers[0, rows]
        for l in range(1, NS):
            force = force + found[l] * layers[l, rows]
        for i, f in enumerate(found + [force]):
            prof[i, rows] = f


def received_rows(count):
    upper = iota((SUB, LANES), 0) < HALO
    gx = lax.axis_index("gx")
    odd = gx % 2 == 1
    keep = (upper & (gx < count - 1)) | (~upper & (gx > 0))

    def halves(first, second, j, cols):
        a, b = first[j, :, cols], second[j, :, cols]
        high, low = jnp.where(odd, b, a), jnp.where(odd, a, b)
        one, two = jnp.where(upper, high, half_swap(low)), jnp.where(upper, half_swap(high), low)
        return jnp.where(keep, one, 0.0), jnp.where(keep, two, 0.0)

    return halves


def pack_columns(ext, plane, count, base, window, tiles, outs, slot):
    lane = iota((window, LANES), 1)
    group = lane // HALO
    groups = LANES // HALO
    packs = [jnp.zeros((window, LANES), F32) for _ in range(2)]
    for l in range(count):
        rows = pl.ds(base, window)
        v = jnp.where(lane < LANES // 2, ext[l + plane, 0, rows], ext[l + plane, tiles - 1, rows])
        v = pltpu.roll(v, HALO * l, 1) if l else v
        packs[l % 2] = jnp.where((group == l) | (group == (l - 1) % groups), v, packs[l % 2])
    even = group % 2 == 0
    low = jnp.where(even, packs[0], packs[1])
    high = jnp.where(even, packs[1], packs[0])
    first_high = lax.axis_index("gy") % 2 == 0
    outs[0][slot] = jnp.where(first_high, high, low)
    outs[1][slot] = jnp.where(first_high, low, high)


def fields_kernel(after, u_ref, k_ref, x0, x1, ext_u, ext_k, out0, out1):
    _, levels, nx, ny = u_ref.shape
    tiles = ny // LANES
    blank = jnp.zeros(ext_u.shape[2:], F32)
    for t in range(tiles + 1):
        for ext in (ext_u, ext_k):
            ext[0, t] = blank
            ext[levels + 1, t] = blank
    halves = received_rows(lax.axis_size("gx"))
    chunks = nx // SUB + 1

    def level(l, _):
        for t in range(tiles):
            cols = slice(t * LANES, (t + 1) * LANES)
            halo = halves(x0, x1, l, cols)
            for c in range(chunks):
                rows = slice(SUB * c, SUB * c + SUB)
                u, k = halo if c == chunks - 1 else (u_ref[0, l, rows, cols], k_ref[0, l, rows, cols])
                store(ext_u, l + 1, t, c, chunks, u)
                store(ext_k, l + 1, t, c, chunks, k * (0.5 + 0.25 * jnp.tanh(u)))
        return 0

    lax.fori_loop(0, levels, level, 0, unroll=2)
    for slot, ext in enumerate((ext_u, ext_k)):
        pack_columns(ext, 1, levels, SUB, nx + SUB, tiles, (out0, out1), slot)


def split(v):
    hi = v.astype(jnp.bfloat16)
    lo = (v - hi.astype(F32)).astype(jnp.bfloat16)
    return hi, lo


def source_kernel(rows_ref, part_ref, w_ref, prof, surf_ref, flux_ref, src_ref, out0, out1, picked):
    _, nx, ny = part_ref.shape
    first = lax.axis_index("comp") == 0
    odd = lax.axis_index("gx") % 2 == 1
    for x in range(nx):
        r = rows_ref[0, x]
        picked[:, pl.ds(x, 1), :] = part_ref[:, pl.ds(r, 1), :]
    forces = []
    for b in range(ny // PATCH):
        cols = slice(b * PATCH, (b + 1) * PATCH)
        x_hi, x_lo = split(picked[:, :, cols].reshape(NS * nx, PATCH))
        w_hi, w_lo = split(w_ref[0, cols, :])
        dims = (((1,), (1,)), ((), ()))
        y = lax.dot_general(x_hi, w_lo, dims, preferred_element_type=F32)
        y = y + lax.dot_general(x_lo, w_hi, dims, preferred_element_type=F32)
        y = y + lax.dot_general(x_hi, w_hi, dims, preferred_element_type=F32)
        y = y.reshape(NS, nx, PATCH)
        total = prof[NS, :, cols] * y[0]
        for l in range(1, NS):
            total = total + prof[NS + l, :, cols] * y[l]
        forces.append(total)
    other_force = jnp.concatenate(forces, axis=1)
    own_force = prof[2 * NS + 2]
    atmos = jnp.where(first, own_force, other_force)
    soil = jnp.where(first, other_force, own_force)
    flux = prof[2 * NS] * (prof[2 * NS + 1] * soil - atmos)
    flux_ref[0] = flux
    signed = jnp.where(first, flux, -flux)
    upper = iota((SUB, ny), 0) < HALO
    src = []
    for l in range(NS):
        s = signed * prof[l]
        if l == 0:
            s = s + surf_ref[0]
        src_ref[l] = s
        src.append(s)
    for j in range(NS // 2):
        a, b = src[2 * j], src[2 * j + 1]
        low = jnp.where(upper, a[:SUB], half_swap(b[:SUB]))
        high = jnp.where(upper, half_swap(a[nx - SUB :]), b[nx - SUB :])
        out0[j] = jnp.where(odd, low, high)
        out1[j] = jnp.where(odd, high, low)


def columns_kernel(s_ref, s0, s1, in0, in1, after, ext_s, out0, out1):
    nx, ny = s_ref.shape[1:]
    tiles = ny // LANES
    halves = received_rows(lax.axis_size("gx"))
    for j in range(NS // 2):
        for t in range(tiles):
            cols = slice(t * LANES, (t + 1) * LANES)
            for i, halo in enumerate(halves(s0, s1, j, cols)):
                ext_s[2 * j + i, t, :nx] = s_ref[2 * j + i, :, cols]
                ext_s[2 * j + i, t, nx:] = halo
    pack_columns(ext_s, 0, NS, 0, nx + SUB, tiles, (out0, out1), 2)


def coefficients_kernel(lo, hi, after, ext_u, ext_k, *refs):
    r, cz, cx, cy, cy_low, diag, beyond = refs[-7:]
    tiles = ext_u.shape[1] - 1
    gx, ngx = lax.axis_index("gx"), lax.axis_size("gx")
    chunks = ext_u.shape[2] // SUB - 2
    few = steps(hi - lo, 6)
    own = range(tiles)
    lane, row = iota((SUB, LANES), 1), iota((SUB, LANES), 0)
    at_end, at_start = lane == LANES - 1, lane == 0
    keep = ((row < HALO) & (gx < ngx - 1)) | ((row >= HALO) & (gx > 0))

    def beside(vs):
        up = [pltpu.roll(v, LANES - 1, 1) for v in vs] + [0.0]
        down = [0.0] + [pltpu.roll(v, 1, 1) for v in vs]
        ups = [jnp.where(at_end, up[t + 1], up[t]) for t in own]
        downs = [jnp.where(at_start, down[t], down[t + 1]) for t in own]
        return ups, downs, jnp.where(at_end, up[0], down[tiles])

    def prepare(j, _):
        first = lo + j * few
        for c in range(chunks):
            at = SUB + SUB * c
            rows = pl.ds(at, SUB)

            def load(ext, plane, dx=0):
                return [ext[first + plane, t, pl.ds(at + dx, SUB)] for t in own]

            k_last, u_last = load(ext_k, 0), load(ext_u, 0)
            k, u = load(ext_k, 1), load(ext_u, 1)
            below = [k[t] + k_last[t] for t in own]
            for i in range(few):
                l = first + i
                k_next, u_next = load(ext_k, i + 2), load(ext_u, i + 2)
                ks = [load(ext_k, i + 1, dx) for dx in (1, -1)]
                us = [load(ext_u, i + 1, dx) for dx in (1, -1)]
                yk, yu = beside(k), beside(u)
                beyond[0, l, rows] = yk[2]
                beyond[1, l, rows] = yu[2]
                above = [k[t] + k_next[t] for t in own]
                for t in own:
                    y_up, y_down = yk[0][t] + k[t], yk[1][t] + k[t]
                    x_up, x_down = ks[0][t] + k[t], ks[1][t] + k[t]
                    total = ((y_up + y_down) + (x_up + x_down)) + (above[t] + below[t])
                    flow = (y_up * yu[0][t] + y_down * yu[1][t]) + (x_up * us[0][t] + x_down * us[1][t])
                    flow = flow + (above[t] * u_next[t] + below[t] * u_last[t])
                    flow = flow - total * u[t]
                    if c == chunks - 1:
                        flow = jnp.where(keep, flow, 0.0)
                    cy[l, t, rows] = y_up
                    cy_low[l, t, rows] = y_down
                    store(cx, l, t, c, chunks, x_up)
                    cz[l, t, rows] = below[t]
                    diag[l, t, rows] = total
                    store(r, l + 1, t, c, chunks, flow)
                k_last, u_last, k, u, below = k, u, k_next, u_next, above
        return 0

    lax.fori_loop(0, (hi - lo) // few, prepare, 0)


def chain_kernel(
    storage_ref, ext_u_in, ext_k, ext_s, y0, y1, flux, beyond, r_in, cz_in, cx_in, cy_in, cy_low_in, diag_in,
    ext_u, p1, p2, moments, flux_out, r, cz, cx, cy, cy_low, diag,
    inside, sem,
):
    flux_copy = pltpu.make_async_copy(flux, flux_out, sem)
    flux_copy.start()
    levels = ext_u.shape[0] - 2
    tiles, all_rows = ext_u.shape[1] - 1, ext_u.shape[2]
    nx = all_rows - 3 * SUB
    window = nx + SUB
    chunks = window // SUB
    gx, gy, ngx, ngy = lax.axis_index("gx"), lax.axis_index("gy"), lax.axis_size("gx"), lax.axis_size("gy")
    odd = gy % 2 == 1
    has_low, has_high = gy > 0, gy < ngy - 1
    even = (iota((window, LANES), 1) // HALO) % 2 == 0

    def halves(f):
        a, b = y0[f], y1[f]
        high = jnp.where(has_high, jnp.where(odd, b, a), 0.0)
        low = jnp.where(has_low, jnp.where(odd, a, b), 0.0)
        return jnp.where(even, high, low), jnp.where(even, low, high)

    def third(packed, l):
        turn = (LANES - HALO * l) % LANES
        return pltpu.roll(packed[l % 2], turn, 1) if turn else packed[l % 2]

    zero_tile = jnp.zeros((SUB, LANES), F32)
    for f, ext in enumerate((ext_u, ext_k)):
        packed = halves(f)
        for l in range(levels):
            columns = third(packed, l)
            for c in range(chunks):
                store(ext, l + 1, tiles, c, chunks, columns[SUB * c : SUB * c + SUB])
    blank = jnp.zeros((all_rows, LANES), F32)
    for t in range(tiles + 1):
        for ext in (r, p1, p2):
            ext[0, t] = blank
            ext[levels + 1, t] = blank

    row, col = iota((SUB, LANES), 0), iota((SUB, LANES), 1)
    row_ok = ((row < HALO) & (gx < ngx - 1)) | ((row >= HALO) & (gx > 0))
    col_ok = ((col < HALO) & has_high) | ((col >= LANES - HALO) & has_low)
    inside[0] = jnp.where(row_ok, 1.0, 0.0)
    inside[1] = jnp.where(col_ok, 1.0, 0.0)
    inside[2] = jnp.where(row_ok & col_ok, 1.0, 0.0)

    lane8 = iota((SUB, LANES), 1)
    at_end, at_start = lane8 == LANES - 1, lane8 == 0

    def beside(vs):
        n = len(vs)
        up = [pltpu.roll(v, LANES - 1, 1) for v in vs]
        down = [pltpu.roll(v, 1, 1) for v in vs]
        ups = [jnp.where(at_end, up[(t + 1) % n], up[t]) for t in range(n)]
        downs = [jnp.where(at_start, down[(t - 1) % n], down[t]) for t in range(n)]
        return ups, downs

    def masked(w, t, chunk):
        if t == tiles:
            return w * inside[2 if chunk == chunks - 1 else 1]
        if chunk == chunks - 1:
            return w * inside[0]
        return w

    shift = storage_ref[0] - CENTRE
    every = range(tiles + 1)
    few = steps(levels, 30)
    many = steps(levels, 15)

    def prepare(j, _):
        first = j * few
        for c in range(chunks):
            at = SUB + SUB * c
            rows = pl.ds(at, SUB)

            def load(ext, plane, dx=0):
                return ext[first + plane, tiles, pl.ds(at + dx, SUB)]

            k_last, u_last = load(ext_k, 0), load(ext_u, 0)
            k, u = load(ext_k, 1), load(ext_u, 1)
            below = k + k_last
            for i in range(few):
                l = first + i
                k_next, u_next = load(ext_k, i + 2), load(ext_u, i + 2)
                edge = [[ext[l + 1, t, rows] for ext in (ext_k, ext_u)] for t in (0, tiles - 1)]
                k_up, u_up = pltpu.roll(k, LANES - 1, 1), pltpu.roll(u, LANES - 1, 1)
                k_down, u_down = pltpu.roll(k, 1, 1), pltpu.roll(u, 1, 1)
                k_own, u_own = beyond[0, l, rows], beyond[1, l, rows]
                y_up = k + jnp.where(at_end, k_own, k_up)
                y_down = k + jnp.where(at_start, k_own, k_down)
                x_up, x_down = k + load(ext_k, i + 1, 1), k + load(ext_k, i + 1, -1)
                above = k + k_next
                total = ((y_up + y_down) + (x_up + x_down)) + (above + below)
                flow = y_up * jnp.where(at_end, u_own, u_up) + y_down * jnp.where(at_start, u_own, u_down)
                flow = flow + (x_up * load(ext_u, i + 1, 1) + x_down * load(ext_u, i + 1, -1))
                flow = flow + (above * u_next + below * u_last)
                cy[l, tiles, rows] = y_up
                cy_low[l, tiles, rows] = y_down
                store(cx, l, tiles, c, chunks, x_up)
                cz[l, tiles, rows] = below
                diag[l, tiles, rows] = total + shift
                store(r, l + 1, tiles, c, chunks, masked(flow - total * u, tiles, c))
                for t, (ko, uo), here, kn, un, face in (
                    (0, edge[0], at_start, k_down, u_down, cy_low),
                    (tiles - 1, edge[1], at_end, k_up, u_up, cy),
                ):
                    kn, un = jnp.where(here, kn, 0.0), jnp.where(here, un, 0.0)
                    face[l, t, rows] = face[l, t, rows] + kn
                    diag[l, t, rows] = diag[l, t, rows] + (kn + shift)
                    store(r, l + 1, t, c, chunks, r[l + 1, t, rows] + ((ko + kn) * un - kn * uo))
                k_last, u_last, k, u, below = k, u, k_next, u_next, above
        return 0

    lax.fori_loop(0, levels // few, prepare, 0)
    for c in range(chunks):
        for t in every:
            cz[levels, t, SUB + SUB * c : 2 * SUB + SUB * c] = zero_tile
    packed = halves(2)
    for l in range(NS):
        columns = third(packed, l)
        for c in range(chunks):
            rows = slice(SUB * c, SUB * c + SUB)
            for t in every:
                extra = columns[rows] if t == tiles else ext_s[l, t, rows]
                store(r, l + 1, t, c, chunks, r[l + 1, t, SUB + SUB * c : 2 * SUB + SUB * c] + extra)

    def operator(src, l, at, outs, unroll):
        rows = pl.ds(at, SUB)
        planes = [[src[l + i, t, rows] for t in every] for i in range(unroll + 2)]
        faces = [[cz[l + i, t, rows] for t in outs] for i in range(unroll + 1)]
        for i in range(unroll):
            v = planes[i + 1]
            v_up, v_down = beside(v)
            ws = []
            for t in outs:
                z = faces[i + 1][t] * planes[i + 2][t] + faces[i][t] * planes[i][t]
                x = cx[l + i, t, rows] * src[l + i + 1, t, pl.ds(at + 1, SUB)]
                x = x + cx[l + i, t, pl.ds(at - 1, SUB)] * src[l + i + 1, t, pl.ds(at - 1, SUB)]
                y = cy[l + i, t, rows] * v_up[t] + cy_low[l + i, t, rows] * v_down[t]
                ws.append((diag[l + i, t, rows] * v[t] - z) - (x + y))
            yield i, v, ws

    def apply(src, dst):
        def step(j, _):
            l = j * many
            for c in range(chunks):
                for i, _, ws in operator(src, l, SUB + SUB * c, every, many):
                    for t, w in enumerate(ws):
                        store(dst, l + i + 1, t, c, chunks, masked(w, t, c))
            return 0

        lax.fori_loop(0, levels // many, step, 0)

    apply(r, p1)
    apply(p1, p2)

    def last(j, sums):
        l = j * many
        sums = list(sums)
        for c in range(nx // SUB):
            at = SUB + SUB * c
            for i, v, ws in operator(p2, l, at, range(tiles), many):
                for t in range(tiles):
                    rows = pl.ds(at, SUB)
                    a, b, w = r[l + i + 1, t, rows], p1[l + i + 1, t, rows], ws[t]
                    for q, term in enumerate((a * a, a * b, b * b, b * v[t], v[t] * v[t], v[t] * w, w * w)):
                        sums[q] = sums[q] + term
        return tuple(sums)

    sums = lax.fori_loop(0, levels // many, last, (zero_tile,) * MOMENTS)
    which = iota((SUB, LANES), 0)
    packed = zero_tile
    for i, m in enumerate(sums):
        total = jnp.sum(jnp.sum(m, axis=1, keepdims=True), axis=0, keepdims=True)
        packed = jnp.where(which == i, total, packed)
    moments[...] = packed
    flux_copy.wait()


def add_kernel(*refs):
    *ins, out = refs
    total = ins[0][...]
    for x in ins[1:]:
        total = total + x[...]
    out[...] = total


def update_kernel(*refs):
    *parts, u_ref, r, p1, p2, out, stage, sems = refs
    total = parts[0][...]
    for x in parts[1:]:
        total = total + x[...]
    m = [total[i : i + 1, :] for i in range(MOMENTS)]

    def gram(i, j):
        return m[i + j + 2] + 2.0 * CENTRE * m[i + j + 1] + CENTRE * CENTRE * m[i + j]

    b = [m[i + 1] + CENTRE * m[i] for i in range(ITERS)]
    l00 = jnp.sqrt(gram(0, 0))
    l10 = gram(1, 0) / l00
    l20 = gram(2, 0) / l00
    l11 = jnp.sqrt(gram(1, 1) - l10 * l10)
    l21 = (gram(2, 1) - l20 * l10) / l11
    l22 = jnp.sqrt(gram(2, 2) - l20 * l20 - l21 * l21)
    z0 = b[0] / l00
    z1 = (b[1] - l10 * z0) / l11
    z2 = (b[2] - l20 * z0 - l21 * z1) / l22
    c2 = z2 / l22
    c1 = (z1 - l21 * c2) / l11
    c0 = (z0 - l10 * c1 - l20 * c2) / l00
    _, levels, nx, ny = stage.shape
    c0, c1, c2 = (jnp.broadcast_to(c, (nx, LANES)) for c in (c0, c1, c2))
    pieces = sems.shape[0]
    per = levels // pieces
    copies = []
    for piece in range(pieces):
        lo = piece * per
        n = per if piece < pieces - 1 else levels - lo

        def step(l, _):
            for t in range(ny // LANES):
                rows = slice(SUB, SUB + nx)
                v = u_ref[l + 1, t, rows] + c0 * r[l + 1, t, rows]
                v = v + (c1 * p1[l + 1, t, rows] + c2 * p2[l + 1, t, rows])
                stage[0, l, :, t * LANES : (t + 1) * LANES] = v
            return 0

        lax.fori_loop(lo, lo + n, step, 0, unroll=2)
        copy = pltpu.make_async_copy(stage.at[0, pl.ds(lo, n)], out.at[0, pl.ds(lo, n)], sems.at[piece])
        copy.start()
        copies.append(copy)
    for copy in copies:
        copy.wait()


def step(
    state, conduct, storage, surface_source, plant_type, plant_table, layer_weights, remap_rows, remap_weights
):
    levels, nx, ny = state.shape[1:]
    tiles = ny // LANES
    window = nx + SUB
    edge = pltpu.VMEM((levels, SUB, ny), F32)
    (layers,) = call(layers_kernel, [(NS, nx, ny)], [state], scratch=[pltpu.SemaphoreType.DMA(())], hbm=(0,))
    partner = lax.ppermute(layers, "comp", [(i, i ^ 1) for i in range(lax.axis_size("comp"))])
    x0, x1 = call(
        edges_kernel,
        [(levels, SUB, ny)] * 2,
        [layers, state, conduct],
        scratch=[edge] * 4 + [pltpu.SemaphoreType.DMA((4,))],
        hbm=(1, 2),
    )
    x0, x1 = swap(x0, "gx", 0), swap(x1, "gx", 1)
    table, weights = plant_table.T, layer_weights.transpose(2, 0, 1)
    (prof,) = call(
        profile_kernel,
        [(PROFILES, nx, ny)],
        [table, weights, plant_type, layers],
        scratch=[
            pltpu.SMEM(table.shape, F32),
            pltpu.SMEM(weights.shape, F32),
            pltpu.VMEM(plant_type.shape, jnp.int32),
            pltpu.SemaphoreType.DMA((3,)),
        ],
        hbm=(0, 1, 2),
    )
    flux, src, s0, s1 = call(
        source_kernel,
        [(1, nx, ny), (NS, nx, ny)] + [(NS // 2, SUB, ny)] * 2,
        [remap_rows, partner, remap_weights, prof, surface_source],
        scratch=[pltpu.VMEM((NS, nx, ny), F32)],
        smem=(0,),
    )
    s0, s1 = swap(s0, "gx", 0), swap(s1, "gx", 1)
    ext = (levels + 2, tiles + 1, nx + 3 * SUB, LANES)
    ext_u, ext_k, y0, y1 = call(fields_kernel, [ext, ext] + [(3, window, LANES)] * 2, [src, state, conduct, x0, x1])
    coef = (levels,) + ext[1:]
    shapes = [ext, (levels + 1,) + ext[1:]] + [coef] * 4 + [(2, levels) + ext[2:]]
    middle = levels * EARLY[0] // EARLY[1]
    coefs = call(functools.partial(coefficients_kernel, 0, middle), shapes, [y0, ext_u, ext_k])
    ext_s, y0, y1 = call(
        columns_kernel,
        [(NS, tiles, window, LANES)] + [(3, window, LANES)] * 2,
        [src, s0, s1, y0, y1, coefs[0]],
        alias={3: 1, 4: 2},
    )
    *coefs, beyond = call(
        functools.partial(coefficients_kernel, middle, levels),
        shapes,
        [ext_s, ext_u, ext_k, *coefs],
        alias={3 + i: i for i in range(len(shapes))},
    )
    y0, y1 = swap(y0, "gy", 0), swap(y1, "gy", 1)
    ext_u, p1, p2, moments, flux, r, *_ = call(
        chain_kernel,
        [ext] * 3 + [(SUB, LANES), (1, nx, ny)] + [c.shape for c in coefs],
        [storage, ext_u, ext_k, ext_s, y0, y1, flux, beyond, *coefs],
        scratch=[pltpu.VMEM((3, SUB, LANES), F32), pltpu.SemaphoreType.DMA(())],
        hbm_outs=(4,),
        smem=(0,),
        alias={1: 0, **{8 + i: 5 + i for i in range(len(coefs))}},
    )
    (moments,) = call(add_kernel, [(SUB, LANES)], everyone(moments, "gx"))
    parts = everyone(moments, "gy")
    (new_state,) = call(
        update_kernel,
        [state.shape],
        parts + [ext_u, r, p1, p2],
        scratch=[pltpu.VMEM(state.shape, F32), pltpu.SemaphoreType.DMA((3,))],
        hbm_outs=(0,),
    )
    return new_state, flux


def solution(mesh):
    in_specs = (
        P("comp", None, "gx", "gy"),
        P("comp", None, "gx", "gy"),
        P("comp"),
        P("comp", "gx", "gy"),
        P("comp", "gx", "gy"),
        P(),
        P(),
        P("comp", "gx"),
        P("comp", "gy", None),
    )
    out_specs = (P("comp", None, "gx", "gy"), P("comp", "gx", "gy"))
    return jax.shard_map(step, mesh=mesh, in_specs=in_specs, out_specs=out_specs, check_vma=False)
```
